256 devices in a mesh: row: 8 (over z_lo, x), col: 32 (over z_hi, y, core).
Axes of the slice: x: 4, y: 4, z: 8 (z_hi: 4, z_lo: 2; z = z_hi * 2 + z_lo), core: 2. Of those that a mesh axis runs over, the one named last changes fastest.
Arguments:
- snapshots: bfloat16 [4096, 32768], P(('row', 'col')), may hold values from -16 to 24
- cell_weights: float32 [32768], replicated, may hold values from 0.25 to 4
Outputs:
- correlation: float32 [4096, 4096], P('col', 'row')
The draws below stay inside these ranges and needn't reach their ends.
All inputs are finite; a program needn't handle non-finite values.
Results may differ from the reference program's by a relative error of at most 0.00037.
Values may be sent and summed in bfloat16 or wider, within the bound.
A program may use at most 64 MiB of HBM per device.

```python
import math
import jax
import jax.numpy as jnp
from jax import lax

SNAPS = 4096
CELLS = 32768


def draw_snapshots(key, part):
    keys = jax.random.split(key, 6)
    times = jnp.arange(SNAPS, dtype=jnp.float32)[:, None] / SNAPS
    amplitude = jnp.exp(jax.random.uniform(keys[0], (CELLS,), jnp.float32, jnp.log(0.3), jnp.log(3.0)))
    base = jax.random.uniform(keys[1], (CELLS,), jnp.float32, 0.5, 2.0)
    freqs = jax.random.uniform(keys[2], (8,), jnp.float32, 6.0, 600.0)
    phases = jax.random.uniform(keys[3], (8, CELLS), jnp.float32, 0.0, 6.2831853)
    weights = jax.random.uniform(keys[4], (8, CELLS), jnp.float32, -0.4, 0.4)
    waves = jnp.zeros((SNAPS, CELLS), jnp.float32)
    for index in range(8):
        waves = waves + weights[index][None, :] * jnp.cos(freqs[index] * times + phases[index][None, :])
    noise = 0.5 * jax.random.truncated_normal(keys[5], -4.0, 4.0, (SNAPS, CELLS), jnp.float32)
    drift = 1.0 + 0.3 * times
    values = base[None, :] * drift + amplitude[None, :] * (waves + noise)
    return values.astype(jnp.bfloat16)


def setup_inputs(seed: int = 0) -> dict:
    key_list = jax.random.split(jax.random.key(seed), 3)
    snapshots = draw_snapshots(jax.random.fold_in(key_list[2], 71), 0)
    cell_weights = jnp.clip(jnp.exp(jax.random.uniform(key_list[1], (CELLS,), jnp.float32, math.log(0.25), math.log(4.0))), 0.25, 4.0)
    return {"snapshots": snapshots, "cell_weights": cell_weights}


def reference(snapshots, cell_weights):
    values = snapshots.astype(jnp.float32)
    mean = lax.optimization_barrier(jnp.sum(values, axis=0)) / SNAPS
    total = jnp.sum(cell_weights)
    scaled = ((values - mean[None, :]) * jnp.sqrt(cell_weights / total)[None, :]).astype(jnp.bfloat16)
    wide = scaled.astype(jnp.float32)
    return jnp.dot(wide, wide.T, preferred_element_type=jnp.float32)
```

```python
import functools

import jax
import jax.numpy as jnp
from jax import lax
from jax.experimental import pallas as pl
from jax.experimental.pallas import tpu as pltpu
from jax.sharding import PartitionSpec as P

MESH = pl.DeviceIdType.MESH
YOFF = (0, 3, 1, 2)


def kernel(snaps, cells, x_ref, w_ref, o_ref, S, R, Sc, Rc, part, xbuf, acc, rsb, psx, psy, mean, fac,
           a_s, a_r, ys, yr, fs, fr, xs, xr, gs, gr, pxs, pxr, pys, pyr, cs, cr, rs, rr, ls):
    width = cells // 16
    row, col = lax.axis_index("row"), lax.axis_index("col")
    zlo, x = row // 4, row % 4
    zhi, y, core = col // 8, (col // 2) % 4, col % 2
    p, q = zhi // 2, zhi % 2
    z = zhi * 2 + zlo

    def dev(zlo=zlo, x=x, zhi=zhi, y=y, core=core):
        return (zlo * 4 + x, zhi * 8 + y * 2 + core)

    def xplus(d):
        return (x + d) % 4

    def yplus(d):
        return (y + d) % 4

    def rcopy(src, dst, ssem, rsem, device):
        return pltpu.make_async_remote_copy(src_ref=src, dst_ref=dst, send_sem=ssem, recv_sem=rsem,
                                            device_id=device, device_id_type=MESH)

    barrier = pltpu.get_barrier_semaphore()
    peers = [dev(y=yplus(d)) for d in (1, 2, 3)] + [dev(x=xplus(d)) for d in (1, 2, 3)]
    for dz in range(8):
        for dc in range(2):
            if dz or dc:
                zz = (z + dz) % 8
                peers.append(dev(zlo=zz % 2, zhi=zz // 2, core=(core + dc) % 2))
    for peer in peers:
        pl.semaphore_signal(barrier, inc=1, device_id=peer, device_id_type=MESH)
    pl.semaphore_wait(barrier, len(peers))

    def g_(v):
        return 1 - p if v < 2 else p

    def lo_(v):
        return (q + v) % 2

    sends = []
    me_slot = z * 2 + core
    my_block = S.at[zlo, zhi // 2, zhi % 2, y, pl.ds(pl.multiple_of(core * 16, 16), 16), :]
    for v in range(4):
        zhi_t = 2 * (1 - zlo if v < 2 else zlo) + (q + v) % 2
        for dz in range(2):
            for dc in range(2):
                zlo_t, core_t = (zlo + dz) % 2, (core + dc) % 2
                slab = (zhi_t * 2 + zlo_t) * 2 + core_t
                src = x_ref.at[:, pl.ds(pl.multiple_of(slab * width, width), width)]
                n = v * 4 + dz * 2 + dc
                out = rcopy(src, my_block, a_s.at[n], a_r.at[me_slot], dev(zhi=zhi_t, zlo=zlo_t, core=core_t))
                if v % 2 == 0 and dz == 0 and dc == 0:
                    same = zhi_t == zhi

                    @pl.when(same)
                    def _(src=src):
                        pltpu.make_async_copy(src, my_block, a_r.at[me_slot]).start()

                    @pl.when(jnp.logical_not(same))
                    def _(out=out):
                        out.start()

                    sends.append((out, jnp.logical_not(same)))
                else:
                    out.start()
                    sends.append((out, None))

    total = jnp.sum(w_ref[...])
    scale = jnp.sqrt(w_ref[pl.ds(pl.multiple_of(me_slot * 16, 16), 16), :] / total)
    for j in range(16):
        fac[:, j * 128:(j + 1) * 128] = scale[j:j + 1, :]

    def a_wait(v):
        for h in range(2):
            for c in range(2):
                slot = ((2 * h + lo_(v)) * 2 + g_(v)) * 2 + c
                block = S.at[g_(v), h, lo_(v), y, c * 16:(c + 1) * 16, :]
                rcopy(block, block, a_s.at[0], a_r.at[slot], dev(core=1 - core)).wait_recv()

    def y_own(v):
        unit = S.at[g_(v), :, lo_(v), y]
        for d in range(2):
            c = rcopy(unit, unit, ys.at[v, d], yr.at[v, d], dev(y=yplus(1 if d == 0 else 3)))
            c.start()
            sends.append((c, None))

    def y_wait(v):
        for d in range(2):
            unit = S.at[g_(v), :, lo_(v), yplus(3 if d == 0 else 1)]
            rcopy(unit, unit, ys.at[v, d], yr.at[v, d], dev(y=yplus(1))).wait_recv()
            half = S.at[g_(v), d, lo_(v), yplus(3 if d == 0 else 1)]
            c = rcopy(half, half, fs.at[v, d], fr.at[v, d], dev(y=yplus(1 if d == 0 else 3)))
            c.start()
            sends.append((c, None))

    def y_last(v):
        for d in range(2):
            half = S.at[g_(v), d, lo_(v), yplus(2)]
            rcopy(half, half, fs.at[v, d], fr.at[v, d], dev(y=yplus(1))).wait_recv()

    is_src = (x % 2) == (y // 2)
    is_mid = jnp.logical_not(is_src)

    def x_send(v, ks):
        @pl.when(is_src)
        def _():
            for k in ks:
                yy = yplus(YOFF[k])
                for d in range(2):
                    rcopy(S.at[g_(v), y % 2, lo_(v), yy], R.at[g_(v), x // 2, lo_(v), yy],
                          xs.at[v, k, d], xr.at[v, k, d], dev(x=xplus(1 if d == 0 else 3))).start()

    def x_local(v):
        @pl.when(is_src)
        def _():
            pltpu.make_async_copy(S.at[g_(v), y % 2, lo_(v)], R.at[g_(v), x // 2, lo_(v)], ls.at[v]).start()

    def x_fwd(v, ks):
        @pl.when(is_mid)
        def _():
            for k in ks:
                yy = yplus(YOFF[k])
                for d in ((0, 1) if k % 2 == 0 else (1, 0)):
                    unit = R.at[g_(v), xplus(3 if d == 0 else 1) // 2, lo_(v), yy]
                    rcopy(unit, unit, xs.at[v, k, d], xr.at[v, k, d], dev(x=xplus(1))).wait_recv()
                    if k % 2 == d:
                        rcopy(unit, unit, gs.at[v, k], gr.at[v, k], dev(x=xplus(1 if d == 0 else 3))).start()

    def x_last(v):
        @pl.when(is_src)
        def _():
            for k in range(4):
                unit = R.at[g_(v), 1 - x // 2, lo_(v), yplus(YOFF[k])]
                rcopy(unit, unit, gs.at[v, k], gr.at[v, k], dev(x=xplus(1))).wait_recv()
            own = R.at[g_(v), x // 2, lo_(v)]
            pltpu.make_async_copy(own, own, ls.at[v]).wait()

    def psum_own():
        def body(i, carry):
            block = S[i // 4, (i // 2) % 2, i % 2, y].astype(jnp.float32)
            return carry + (block[0:8] + block[8:16]) + (block[16:24] + block[24:32])

        total8 = lax.fori_loop(0, 8, body, jnp.zeros((8, width), jnp.float32))
        psx[x] = jnp.sum(total8, axis=0, keepdims=True)
        for d in (1, 2, 3):
            c = rcopy(psx.at[x], psx.at[x], pxs.at[d - 1], pxr.at[d - 1], dev(x=xplus(d)))
            c.start()
            sends.append((c, None))

    def psum_x():
        for d in (1, 2, 3):
            slot = psx.at[xplus(4 - d)]
            rcopy(slot, slot, pxs.at[d - 1], pxr.at[d - 1], dev(x=xplus(d))).wait_recv()
        psy[y] = (psx[0] + psx[1]) + (psx[2] + psx[3])
        for d in (1, 2, 3):
            c = rcopy(psy.at[y], psy.at[y], pys.at[d - 1], pyr.at[d - 1], dev(y=yplus(d)))
            c.start()
            sends.append((c, None))

    def psum_y():
        for d in (1, 2, 3):
            slot = psy.at[yplus(4 - d)]
            rcopy(slot, slot, pys.at[d - 1], pyr.at[d - 1], dev(y=yplus(d))).wait_recv()
        mean[...] = ((psy[0] + psy[1]) + (psy[2] + psy[3])) / snaps

    a_wait(0)
    y_own(0)
    x_send(0, (0,))
    a_wait(1)
    y_own(1)
    y_wait(0)
    x_send(0, (1, 2))
    a_wait(2)
    y_own(2)
    y_last(0)
    x_send(0, (3,))
    x_local(0)
    x_fwd(0, (0, 1))
    x_send(1, (0,))
    a_wait(3)
    psum_own()
    y_wait(1)
    x_send(1, (1, 2))
    x_fwd(0, (2, 3))
    y_own(3)
    psum_x()
    y_last(1)
    x_send(1, (3,))
    x_local(1)
    x_send(2, (0,))
    y_wait(2)
    x_send(2, (1, 2))
    x_fwd(1, (0, 1))
    psum_y()
    y_last(2)
    x_send(2, (3,))
    x_local(2)
    x_fwd(1, (2, 3))
    x_send(3, (0,))
    y_wait(3)
    x_send(3, (1, 2))
    x_fwd(2, (0, 1))
    y_last(3)
    x_send(3, (3,))
    x_local(3)

    def scaled(block):
        return ((block.astype(jnp.float32) - mean[...]) * fac[...]).astype(jnp.bfloat16)

    def scale_s(i, carry):
        Sc[pl.ds(pl.multiple_of(i * 32, 32), 32), :] = scaled(S[i // 16, (i // 8) % 2, (i // 4) % 2, i % 4])
        return carry

    lax.fori_loop(0, 32, scale_s, 0)
    x_fwd(2, (2, 3))
    x_last(0)
    x_last(1)

    def multiply(t):
        g = g_(0 if t < 2 else 2)
        b = (q, 1 - q, 1 - q, q)[t]

        def scale_r(i, carry):
            Rc[pl.ds(pl.multiple_of(i * 32, 32), 32), :] = scaled(R[g, b, i // 4, i % 4])
            return carry

        lax.fori_loop(0, 8, scale_r, 0)

        def dot(zo, carry):
            part[t, zo] = lax.dot_general(
                Rc[...], Sc[pl.ds(pl.multiple_of(zo * 512, 512), 512), :],
                (((1,), (1,)), ((), ())), preferred_element_type=jnp.float32)
            return carry

        lax.fori_loop(0, 2, dot, 0)
        c = rcopy(part.at[t, :, pl.ds(pl.multiple_of((1 - core) * 128, 128), 128), :], xbuf.at[t],
                  cs.at[t], cr.at[t], dev(core=1 - core))
        c.start()
        sends.append((c, None))

    def reduce(t):
        rcopy(xbuf.at[t], xbuf.at[t], cs.at[t], cr.at[t], dev(core=1 - core)).wait_recv()
        acc[t] = part[t, :, pl.ds(pl.multiple_of(core * 128, 128), 128), :] + xbuf[t]
        g = g_(0 if t < 2 else 2)
        zhi_t = 2 * g + (q, 1 - q, 1 - q, q)[t]
        for n in range(2 if t < 3 else 1):
            zlo_t = n if t < 3 else 1 - zlo
            c = rcopy(acc.at[t, zlo_t], rsb.at[z], rs.at[t * 2 + n], rr.at[z], dev(zhi=zhi_t, zlo=zlo_t))
            c.start()
            sends.append((c, None))

    multiply(0)
    multiply(1)
    reduce(0)
    reduce(1)
    x_fwd(3, (0, 1, 2, 3))
    x_last(2)
    x_last(3)
    multiply(2)
    multiply(3)
    reduce(2)
    reduce(3)
    o_ref[...] = acc[3, zlo]
    for d in range(7, 0, -1):
        slot = rsb.at[(z + d) % 8]
        rcopy(slot, slot, rs.at[0], rr.at[(z + d) % 8], dev(core=1 - core)).wait_recv()
        o_ref[...] += slot[...]

    for c, cond in sends:
        if cond is None:
            c.wait_send()
        else:
            @pl.when(cond)
            def _(c=c):
                c.wait_send()

    @pl.when(is_src)
    def _():
        for v in range(4):
            for k in range(4):
                unit = S.at[0, 0, 0, 0]
                for d in range(2):
                    rcopy(unit, unit, xs.at[v, k, d], xr.at[v, k, d], dev(x=xplus(1))).wait_send()

    @pl.when(is_mid)
    def _():
        for v in range(4):
            for k in range(4):
                unit = R.at[0, 0, 0, 0]
                rcopy(unit, unit, gs.at[v, k], gr.at[v, k], dev(x=xplus(1))).wait_send()


def solution(mesh):
    def on_device(snapshots, cell_weights):
        per_device, cells = snapshots.shape
        snaps = per_device * mesh.shape["row"] * mesh.shape["col"]
        width = cells // 16
        dma, bf16, f32 = pltpu.SemaphoreType.DMA, jnp.bfloat16, jnp.float32
        V = pltpu.VMEM
        return pl.pallas_call(
            functools.partial(kernel, snaps, cells),
            out_shape=jax.ShapeDtypeStruct((128, 512), f32),
            in_specs=[pl.BlockSpec(memory_space=pl.ANY), pl.BlockSpec(memory_space=V)],
            out_specs=pl.BlockSpec(memory_space=V),
            scratch_shapes=[
                V((2, 2, 2, 4, 32, width), bf16),
                V((2, 2, 2, 4, 32, width), bf16),
                V((1024, width), bf16),
                V((256, width), bf16),
                V((4, 2, 256, 512), f32),
                V((4, 2, 128, 512), f32),
                V((4, 2, 128, 512), f32),
                V((8, 128, 512), f32),
                V((4, 1, width), f32),
                V((4, 1, width), f32),
                V((1, width), f32),
                V((1, width), f32),
                dma((16,)), dma((16,)),
                dma((4, 2)), dma((4, 2)), dma((4, 2)), dma((4, 2)),
                dma((4, 4, 2)), dma((4, 4, 2)), dma((4, 4)), dma((4, 4)),
                dma((3,)), dma((3,)), dma((3,)), dma((3,)),
                dma((4,)), dma((4,)), dma((8,)), dma((8,)), dma((4,)),
            ],
            compiler_params=pltpu.CompilerParams(
                collective_id=0, has_side_effects=True, vmem_limit_bytes=60 * 1024 * 1024),
        )(snapshots, cell_weights.reshape(cells // 128, 128))

    return jax.shard_map(
        on_device,
        mesh=mesh,
        in_specs=(P(("row", "col"), None), P()),
        out_specs=P("col", "row"),
        check_vma=False,
    )
```

```python
import functools

import jax
import jax.numpy as jnp
from jax import lax
from jax.experimental import pallas as pl
from jax.experimental.pallas import tpu as pltpu
from jax.sharding import PartitionSpec as P

MESH = pl.DeviceIdType.MESH
YOFF = (0, 3, 1, 2)
PARTS = 2
ROUNDS = 4 * PARTS


def kernel(snaps, cells, x_ref, w_hbm, o_ref, S, R, Sc, Rc, part, xbuf, up, down, psx, psy, mean, fac, w_ref,
           a_s, a_r, ys, yr, fs, fr, xs, xr, gs, gr, pxs, pxr, pys, pyr, cs, cr, us, ur, ds, dr, ls, ws):
    width = cells // 16 // PARTS
    row, col = lax.axis_index("row"), lax.axis_index("col")
    zlo, x = row // 4, row % 4
    zhi, y, core = col // 8, (col // 2) % 4, col % 2
    z = zhi * 2 + zlo
    is_src = (x % 2) == (y // 2)
    is_mid = jnp.logical_not(is_src)

    def dev(z=z, x=x, y=y, core=core):
        return ((z % 2) * 4 + x, (z // 2) * 8 + y * 2 + core)

    def xplus(d):
        return (x + d) % 4

    def yplus(d):
        return (y + d) % 4

    def zplus(d):
        return (z + d) % 8

    def side(d):
        return 1 if d == 0 else 3

    def rcopy(src, dst, ssem, rsem, device):
        return pltpu.make_async_remote_copy(src_ref=src, dst_ref=dst, send_sem=ssem, recv_sem=rsem,
                                            device_id=device, device_id_type=MESH)

    def got(ref, rsem):
        rcopy(ref, ref, a_s.at[0, 0], rsem, dev(core=1 - core)).wait_recv()

    def left(ref, ssem):
        rcopy(ref, ref, ssem, a_r.at[0, 0], dev(core=1 - core)).wait_send()

    sends = []

    def go(c):
        c.start()
        sends.append(c)

    weights = pltpu.make_async_copy(w_hbm, w_ref, ws)
    weights.start()

    barrier = pltpu.get_barrier_semaphore()
    peers = [dev(y=yplus(d)) for d in (1, 2, 3)] + [dev(x=xplus(d)) for d in (1, 2, 3)]
    for dz in range(8):
        for dc in range(2):
            if dz or dc:
                peers.append(dev(z=zplus(dz), core=(core + dc) % 2))
    for peer in peers:
        pl.semaphore_signal(barrier, inc=1, device_id=peer, device_id_type=MESH)
    pl.semaphore_wait(barrier, len(peers))

    def order(w):
        part_of, v = w // 4, w % 4
        m = (z + (0, 1, 3, 2)[v]) % 4 if part_of < PARTS - 1 else v
        return part_of, m % 2, m // 2

    me_slot = z * 2 + core
    for k in range(PARTS):
        block = S.at[k, zlo, zhi // 2, zhi % 2, y, pl.ds(pl.multiple_of(core * 16, 16), 16), :]
        for n, dz in enumerate((0, 4, 7, 3, 1, 5, 6, 2)):
            for dc in range(2):
                z_t, core_t = zplus(dz), (core + dc) % 2
                first = (z_t * 2 + core_t) * (width * PARTS) + k * width
                src = x_ref.at[:, pl.ds(pl.multiple_of(first, width), width)]
                if dz == 0 and dc == 0:
                    pltpu.make_async_copy(src, block, a_r.at[k, me_slot]).start()
                else:
                    go(rcopy(src, block, a_s.at[k, n * 2 + dc], a_r.at[k, me_slot], dev(z=z_t, core=core_t)))

    weights.wait()
    total = jnp.sum(w_ref[...])
    scale = jnp.sqrt(w_ref[pl.ds(pl.multiple_of(me_slot * 16, 16), 16), :] / total)
    per = 16 // PARTS
    for j in range(16):
        fac[j // per, :, (j % per) * 128:(j % per + 1) * 128] = scale[j:j + 1, :]

    def a_wait(w):
        k, g, lo = order(w)
        for h in range(2):
            for c in range(2):
                got(S.at[k, g, h, lo, y, c * 16:(c + 1) * 16, :], a_r.at[k, ((2 * h + lo) * 2 + g) * 2 + c])

    def y_own(w):
        k, g, lo = order(w)
        unit = S.at[k, g, :, lo, y]
        for d in range(2):
            go(rcopy(unit, unit, ys.at[w, d], yr.at[w, d], dev(y=yplus(side(d)))))

    def y_wait(w):
        k, g, lo = order(w)
        for d in range(2):
            yy = yplus(4 - side(d))
            got(S.at[k, g, :, lo, yy], yr.at[w, d])
            half = S.at[k, g, d, lo, yy]
            go(rcopy(half, half, fs.at[w, d], fr.at[w, d], dev(y=yplus(side(d)))))

    def y_last(w):
        k, g, lo = order(w)
        for d in range(2):
            got(S.at[k, g, d, lo, yplus(2)], fr.at[w, d])

    def x_send(w, js):
        k, g, lo = order(w)

        @pl.when(is_src)
        def _():
            for j in js:
                yy = yplus(YOFF[j])
                for d in range(2):
                    rcopy(S.at[k, g, y % 2, lo, yy], R.at[k, g, x // 2, lo, yy],
                          xs.at[w, j, d], xr.at[w, j, d], dev(x=xplus(side(d)))).start()

    def x_local(w):
        k, g, lo = order(w)

        @pl.when(is_src)
        def _():
            pltpu.make_async_copy(S.at[k, g, y % 2, lo], R.at[k, g, x // 2, lo], ls.at[w]).start()

    def x_fwd(w):
        k, g, lo = order(w)

        @pl.when(is_mid)
        def _():
            for j in range(4):
                yy = yplus(YOFF[j])
                for d in ((0, 1) if j % 2 == 0 else (1, 0)):
                    unit = R.at[k, g, xplus(4 - side(d)) // 2, lo, yy]
                    got(unit, xr.at[w, j, d])
                    if j % 2 == d:
                        rcopy(unit, unit, gs.at[w, j], gr.at[w, j], dev(x=xplus(side(d)))).start()

    def x_last(w):
        k, g, lo = order(w)

        @pl.when(is_src)
        def _():
            for j in range(4):
                got(R.at[k, g, 1 - x // 2, lo, yplus(YOFF[j])], gr.at[w, j])
            own = R.at[k, g, x // 2, lo]
            pltpu.make_async_copy(own, own, ls.at[w]).wait()

    def psum_own(k):
        def body(i, carry):
            block = S[k, i // 4, (i // 2) % 2, i % 2, y].astype(jnp.float32)
            return carry + (block[0:8] + block[8:16]) + (block[16:24] + block[24:32])

        total8 = lax.fori_loop(0, 8, body, jnp.zeros((8, width), jnp.float32))
        psx[k, x] = jnp.sum(total8, axis=0, keepdims=True)
        for d in (1, 2, 3):
            go(rcopy(psx.at[k, x], psx.at[k, x], pxs.at[k, d - 1], pxr.at[k, d - 1], dev(x=xplus(d))))

    def psum_x(k):
        for d in (1, 2, 3):
            got(psx.at[k, xplus(4 - d)], pxr.at[k, d - 1])
        psy[k, y] = (psx[k, 0] + psx[k, 1]) + (psx[k, 2] + psx[k, 3])
        for d in (1, 2, 3):
            go(rcopy(psy.at[k, y], psy.at[k, y], pys.at[k, d - 1], pyr.at[k, d - 1], dev(y=yplus(d))))

    def psum_y(k):
        for d in (1, 2, 3):
            got(psy.at[k, yplus(4 - d)], pyr.at[k, d - 1])
        mean[k] = ((psy[k, 0] + psy[k, 1]) + (psy[k, 2] + psy[k, 3])) / snaps

    def scaled(k, block):
        return ((block.astype(jnp.float32) - mean[k]) * fac[k]).astype(jnp.bfloat16)

    def scale_s(k):
        def body(i, carry):
            Sc[k, pl.ds(pl.multiple_of(i * 32, 32), 32), :] = scaled(k, S[k, i // 16, (i // 8) % 2, (i // 4) % 2, i % 4])
            return carry

        lax.fori_loop(0, 32, body, 0)

    def multiply(w):
        k, g, lo = order(w)

        def body(i, carry):
            Rc[pl.ds(pl.multiple_of(i * 32, 32), 32), :] = scaled(k, R[k, g, i // 4, lo, i % 4])
            return carry

        lax.fori_loop(0, 8, body, 0)

        def dot(zo, carry):
            product = lax.dot_general(
                Rc[...], Sc[k, pl.ds(pl.multiple_of(zo * 512, 512), 512), :],
                (((1,), (1,)), ((), ())), preferred_element_type=jnp.float32)
            if k == 0:
                part[lo, g, zo] = product
            else:
                part[lo, g, zo] += product
            return carry

        lax.fori_loop(0, 2, dot, 0)

    def tr_give(lo, g):
        @pl.when(core == 1 - lo)
        def _():
            rcopy(part.at[lo, g], xbuf.at[g], cs.at[g], cr.at[g], dev(core=1 - core)).start()

    def piece(dz, half):
        zz = zplus(dz)
        return part.at[core, zz // 4, zz % 2, pl.ds(pl.multiple_of((zz // 2) % 2 * 128 + half * 64, 64), 64), :]

    def tr_send(steps, half, upward):
        ss, sr, buf = (us, ur, up) if upward else (ds, dr, down)
        slot = buf.at[steps - 1, half]
        rcopy(piece(steps if upward else 8 - steps, half), slot, ss.at[steps - 1, half], sr.at[steps - 1, half],
              dev(z=zplus(1 if upward else 7))).start()

    def tr_add(steps, half, upward):
        sr, buf = (ur, up) if upward else (dr, down)
        got(buf.at[steps, half], sr.at[steps, half])
        mine = piece(steps if upward else (8 - steps) % 8, half)
        mine[...] += buf[steps, half]

    def tr_start(lo):
        @pl.when(core == lo)
        def _():
            for g in range(2):
                got(xbuf.at[g], cr.at[g])
                part[core, g] += xbuf[g]
            tr_send(4, 0, True)
            tr_send(4, 1, False)
            tr_send(3, 1, True)
            tr_send(3, 0, False)

    def tr_step(lo, steps):
        @pl.when(core == lo)
        def _():
            tr_add(steps, 0, True)
            tr_send(steps, 0, True)
            tr_add(steps, 1, False)
            tr_send(steps, 1, False)
            if steps > 1:
                tr_add(steps - 1, 1, True)
                tr_send(steps - 1, 1, True)
                tr_add(steps - 1, 0, False)
                tr_send(steps - 1, 0, False)

    def tr_end(lo):
        @pl.when(core == lo)
        def _():
            zo, base = zlo, (z // 2) % 2 * 128
            for half in (1, 0):
                got(up.at[0, half], ur.at[0, half])
                got(down.at[0, 1 - half], dr.at[0, 1 - half])
            for half in range(2):
                mine = part[core, z // 4, zo, pl.ds(pl.multiple_of(base + half * 64, 64), 64), :]
                o_ref[half * 64:(half + 1) * 64, :] = mine + up[0, half] + down[0, half]

    a_wait(0)
    y_own(0)
    x_send(0, (0,))
    a_wait(1)
    y_own(1)
    x_send(1, (0,))
    y_wait(0)
    x_send(0, (1, 2))
    a_wait(2)
    y_own(2)
    x_send(2, (0,))
    y_wait(1)
    x_send(1, (1, 2))
    y_last(0)
    x_send(0, (3,))
    x_local(0)
    a_wait(3)
    psum_own(0)
    y_own(3)
    x_send(3, (0,))
    y_wait(2)
    x_send(2, (1, 2))
    x_fwd(0)
    y_last(1)
    x_send(1, (3,))
    x_local(1)
    a_wait(4)
    y_own(4)
    x_send(4, (0,))
    y_wait(3)
    x_send(3, (1, 2))
    x_fwd(1)
    y_last(2)
    x_send(2, (3,))
    x_local(2)
    psum_x(0)
    a_wait(5)
    y_own(5)
    x_send(5, (0,))
    y_wait(4)
    x_send(4, (1, 2))
    x_fwd(2)
    y_last(3)
    x_send(3, (3,))
    x_local(3)
    a_wait(6)
    y_own(6)
    a_wait(7)
    psum_own(1)
    x_send(6, (0,))
    y_wait(5)
    x_send(5, (1, 2))
    psum_y(0)
    scale_s(0)
    y_last(4)
    x_send(4, (3,))
    x_local(4)
    x_fwd(3)
    y_own(7)
    x_send(7, (0,))
    y_wait(6)
    x_send(6, (1, 2))
    x_last(0)
    multiply(0)
    y_last(5)
    x_send(5, (3,))
    x_local(5)
    psum_x(1)
    x_fwd(4)
    y_wait(7)
    x_send(7, (1, 2))
    x_last(1)
    multiply(1)
    y_last(6)
    x_send(6, (3,))
    x_local(6)
    x_last(2)
    multiply(2)
    x_fwd(5)
    y_last(7)
    x_send(7, (3,))
    x_local(7)
    x_last(3)
    multiply(3)
    psum_y(1)
    scale_s(1)
    x_last(4)
    multiply(4)
    tr_give(0, 0)
    x_last(5)
    multiply(5)
    tr_give(0, 1)
    x_fwd(6)
    tr_start(0)
    x_last(6)
    multiply(6)
    tr_give(1, 0)
    tr_step(0, 3)
    x_fwd(7)
    x_last(7)
    multiply(7)
    tr_give(1, 1)
    tr_step(0, 2)
    tr_start(1)
    tr_step(0, 1)
    tr_step(1, 3)
    tr_step(1, 2)
    tr_step(1, 1)
    tr_end(0)
    tr_end(1)

    for c in sends:
        c.wait_send()
    unit = S.at[0, 0, 0, 0, 0]

    @pl.when(is_src)
    def _():
        for w in range(ROUNDS):
            for j in range(4):
                for d in range(2):
                    left(unit, xs.at[w, j, d])

    @pl.when(is_mid)
    def _():
        for w in range(ROUNDS):
            for j in range(4):
                left(unit, gs.at[w, j])

    for g in range(2):
        left(xbuf.at[g], cs.at[g])
    for steps in range(4):
        for half in range(2):
            if steps < 3 or half == 0:
                left(up.at[0, 0], us.at[steps, half])
            if steps < 3 or half == 1:
                left(up.at[0, 0], ds.at[steps, half])


def solution(mesh):
    def on_device(snapshots, cell_weights):
        per_device, cells = snapshots.shape
        snaps = per_device * mesh.shape["row"] * mesh.shape["col"]
        width = cells // 16 // PARTS
        dma, bf16, f32 = pltpu.SemaphoreType.DMA, jnp.bfloat16, jnp.float32
        V = pltpu.VMEM
        return pl.pallas_call(
            functools.partial(kernel, snaps, cells),
            out_shape=jax.ShapeDtypeStruct((128, 512), f32),
            in_specs=[pl.BlockSpec(memory_space=pl.ANY), pl.BlockSpec(memory_space=pl.ANY)],
            out_specs=pl.BlockSpec(memory_space=V),
            scratch_shapes=[
                V((PARTS, 2, 2, 2, 4, 32, width), bf16),
                V((PARTS, 2, 2, 2, 4, 32, width), bf16),
                V((PARTS, 1024, width), bf16),
                V((256, width), bf16),
                V((2, 2, 2, 256, 512), f32),
                V((2, 2, 256, 512), f32),
                V((4, 2, 64, 512), f32),
                V((4, 2, 64, 512), f32),
                V((PARTS, 4, 1, width), f32),
                V((PARTS, 4, 1, width), f32),
                V((PARTS, 1, width), f32),
                V((PARTS, 1, width), f32),
                V((cells // 128, 128), f32),
                dma((PARTS, 16)), dma((PARTS, 16)),
                dma((ROUNDS, 2)), dma((ROUNDS, 2)), dma((ROUNDS, 2)), dma((ROUNDS, 2)),
                dma((ROUNDS, 4, 2)), dma((ROUNDS, 4, 2)), dma((ROUNDS, 4)), dma((ROUNDS, 4)),
                dma((PARTS, 3)), dma((PARTS, 3)), dma((PARTS, 3)), dma((PARTS, 3)),
                dma((2,)), dma((2,)), dma((4, 2)), dma((4, 2)), dma((4, 2)), dma((4, 2)), dma((ROUNDS,)), dma,
            ],
            compiler_params=pltpu.CompilerParams(
                collective_id=0, has_side_effects=True, vmem_limit_bytes=60 * 1024 * 1024),
        )(snapshots, cell_weights.reshape(cells // 128, 128))

    return jax.shard_map(
        on_device,
        mesh=mesh,
        in_specs=(P(("row", "col"), None), P()),
        out_specs=P("col", "row"),
        check_vma=False,
    )
```

```python
import functools

import jax
import jax.numpy as jnp
from jax import lax
from jax.experimental import pallas as pl
from jax.experimental.pallas import tpu as pltpu
from jax.sharding import PartitionSpec as P

MESH = pl.DeviceIdType.MESH
YOFF = (0, 3, 1, 2)
PARTS = 2
ROUNDS = 4 * PARTS


def kernel(snaps, cells, x_ref, w_hbm, o_ref, S, R, Sc, Rc, part, xbuf, up, down, psx, psy, mean, fac, w_ref,
           a_s, a_r, ys, yr, fs, fr, xs, xr, gs, gr, pxs, pxr, pys, pyr, cs, cr, us, ur, ds, dr, ls, ws):
    width = cells // 16 // PARTS
    row, col = lax.axis_index("row"), lax.axis_index("col")
    zlo, x = row // 4, row % 4
    zhi, y, core = col // 8, (col // 2) % 4, col % 2
    z = zhi * 2 + zlo
    is_src = (x % 2) == (y // 2)
    is_mid = jnp.logical_not(is_src)

    def dev(z=z, x=x, y=y, core=core):
        return ((z % 2) * 4 + x, (z // 2) * 8 + y * 2 + core)

    def xplus(d):
        return (x + d) % 4

    def yplus(d):
        return (y + d) % 4

    def zplus(d):
        return (z + d) % 8

    def side(d):
        return 1 if d == 0 else 3

    def rcopy(src, dst, ssem, rsem, device):
        return pltpu.make_async_remote_copy(src_ref=src, dst_ref=dst, send_sem=ssem, recv_sem=rsem,
                                            device_id=device, device_id_type=MESH)

    def got(ref, rsem):
        rcopy(ref, ref, a_s, rsem, dev(core=1 - core)).wait_recv()

    def left(ref, ssem):
        rcopy(ref, ref, ssem, a_r.at[0, 0], dev(core=1 - core)).wait_send()

    sends = []

    weights = pltpu.make_async_copy(w_hbm, w_ref, ws)
    weights.start()

    barrier = pltpu.get_barrier_semaphore()
    peers = [dev(y=yplus(d)) for d in (1, 2, 3)] + [dev(x=xplus(d)) for d in (1, 2, 3)]
    for dz in range(8):
        for dc in range(2):
            if dz or dc:
                peers.append(dev(z=zplus(dz), core=(core + dc) % 2))

    def barrier_all():
        for peer in peers:
            pl.semaphore_signal(barrier, inc=1, device_id=peer, device_id_type=MESH)
        pl.semaphore_wait(barrier, len(peers))

    barrier_all()

    def order(w):
        part_of, v = w // 4, w % 4
        m = (z + (0, 1, 3, 2)[v]) % 4 if part_of < PARTS - 1 else v
        return part_of, m % 2, m // 2

    me_slot = z * 2 + core

    def tr_cells(k):
        block = S.at[k, zlo, zhi // 2, zhi % 2, y, pl.ds(pl.multiple_of(core * 16, 16), 16), :]
        for dz in (0, 4, 7, 3, 1, 5, 6, 2):
            for dc in range(2):
                z_t, core_t = zplus(dz), (core + dc) % 2
                first = (z_t * 2 + core_t) * (width * PARTS) + k * width
                src = x_ref.at[:, pl.ds(pl.multiple_of(first, width), width)]
                if dz == 0 and dc == 0:
                    pltpu.make_async_copy(src, block, a_r.at[k, z % 4]).start()
                else:
                    rcopy(src, block, a_s, a_r.at[k, z % 4], dev(z=z_t, core=core_t)).start()

    tr_cells(0)
    tr_cells(1)

    def tr_weights():
        weights.wait()
        total = jnp.sum(w_ref[...])
        scale = jnp.sqrt(w_ref[pl.ds(pl.multiple_of(me_slot * 16, 16), 16), :] / total)
        per = 16 // PARTS
        for j in range(16):
            fac[j // per, :, (j % per) * 128:(j % per + 1) * 128] = scale[j:j + 1, :]

    def a_wait(w):
        k, g, lo = order(w)
        got(S.at[k, g, :, lo, y], a_r.at[k, 2 * lo + g])

    def y_own(w):
        k, g, lo = order(w)
        unit = S.at[k, g, :, lo, y]
        for d in range(2):
            rcopy(unit, unit, ys, yr.at[w, d], dev(y=yplus(side(d)))).start()

    def y_wait(w):
        k, g, lo = order(w)
        for d in range(2):
            yy = yplus(4 - side(d))
            got(S.at[k, g, :, lo, yy], yr.at[w, d])
            half = S.at[k, g, d, lo, yy]
            rcopy(half, half, fs, fr.at[w], dev(y=yplus(side(d)))).start()

    def y_last(w):
        k, g, lo = order(w)
        got(S.at[k, g, :, lo, yplus(2)], fr.at[w])

    def x_send(w, js):
        k, g, lo = order(w)

        @pl.when(is_src)
        def _():
            for j in js:
                yy = yplus(YOFF[j])
                for d in range(2):
                    rcopy(S.at[k, g, y % 2, lo, yy], R.at[k, g, x // 2, lo, yy],
                          xs, xr.at[w, j, d], dev(x=xplus(side(d)))).start()

    def x_rest(w):
        k, g, lo = order(w)

        @pl.when(is_src)
        def _():
            for pos in range(4):
                for d in range(2):
                    j = ((0, 2, 1, 3), (1, 3, 0, 2))[d][pos]
                    yy = yplus(YOFF[j])
                    rcopy(S.at[k, g, y % 2, lo, yy], R.at[k, g, x // 2, lo, yy],
                          xs, xr.at[w, j, d], dev(x=xplus(side(d)))).start()

    def x_local(w):
        k, g, lo = order(w)

        @pl.when(is_src)
        def _():
            pltpu.make_async_copy(S.at[k, g, y % 2, lo], R.at[k, g, x // 2, lo], ls.at[w]).start()

    def x_fwd(w):
        k, g, lo = order(w)

        @pl.when(is_mid)
        def _():
            for n in range(8):
                if w < 6:
                    j, d = n // 2, (n // 2 + n) % 2
                else:
                    d = n % 2
                    j = ((0, 2, 1, 3), (1, 3, 0, 2))[d][n // 2]
                yy = yplus(YOFF[j])
                if True:
                    unit = R.at[k, g, xplus(4 - side(d)) // 2, lo, yy]
                    got(unit, xr.at[w, j, d])
                    if j % 2 == d:
                        rcopy(unit, unit, gs, gr.at[w], dev(x=xplus(side(d)))).start()

    def x_last(w):
        k, g, lo = order(w)

        @pl.when(is_src)
        def _():
            got(R.at[k, g, 1 - x // 2, lo], gr.at[w])
            own = R.at[k, g, x // 2, lo]
            pltpu.make_async_copy(own, own, ls.at[w]).wait()

    def psum_own(k):
        def body(i, carry):
            block = S[k, i // 4, (i // 2) % 2, i % 2, y].astype(jnp.float32)
            return carry + (block[0:8] + block[8:16]) + (block[16:24] + block[24:32])

        total8 = lax.fori_loop(0, 8, body, jnp.zeros((8, width), jnp.float32))
        psx[k, x] = jnp.sum(total8, axis=0, keepdims=True)
        for d in (1, 2, 3):
            c = rcopy(psx.at[k, x], psx.at[k, x], pxs.at[k, d - 1], pxr.at[k, d - 1], dev(x=xplus(d)))
            c.start()
            sends.append(c)

    def psum_x(k):
        for d in (1, 2, 3):
            got(psx.at[k, xplus(4 - d)], pxr.at[k, d - 1])
        psy[k, y] = (psx[k, 0] + psx[k, 1]) + (psx[k, 2] + psx[k, 3])
        for d in (1, 2, 3):
            c = rcopy(psy.at[k, y], psy.at[k, y], pys.at[k, d - 1], pyr.at[k, d - 1], dev(y=yplus(d)))
            c.start()
            sends.append(c)

    def psum_y(k):
        for d in (1, 2, 3):
            got(psy.at[k, yplus(4 - d)], pyr.at[k, d - 1])
        mean[k] = ((psy[k, 0] + psy[k, 1]) + (psy[k, 2] + psy[k, 3])) / snaps

    def scaled(k, block):
        return ((block.astype(jnp.float32) - mean[k]) * fac[k]).astype(jnp.bfloat16)

    def scale_s(k):
        def body(i, carry):
            Sc[k, pl.ds(pl.multiple_of(i * 32, 32), 32), :] = scaled(k, S[k, i // 16, (i // 8) % 2, (i // 4) % 2, i % 4])
            return carry

        lax.fori_loop(0, 32, body, 0)

    def multiply(w):
        k, g, lo = order(w)

        def body(i, carry):
            Rc[pl.ds(pl.multiple_of(i * 32, 32), 32), :] = scaled(k, R[k, g, i // 4, lo, i % 4])
            return carry

        lax.fori_loop(0, 8, body, 0)

        def dot(zo, carry):
            product = lax.dot_general(
                Rc[...], Sc[k, pl.ds(zo * 512 if isinstance(zo, int) else pl.multiple_of(zo * 512, 512), 512), :],
                (((1,), (1,)), ((), ())), preferred_element_type=jnp.float32)
            if k == 0:
                part[lo, g, zo] = product
            else:
                part[lo, g, zo] += product
            return carry

        if k == 0:
            lax.fori_loop(0, 2, dot, 0)
        else:
            for zo in range(2):
                dot(zo, 0)
                give(lo, g, zo)

    def give(lo, g, zo):
        @pl.when(core == 1 - lo)
        def _():
            rcopy(part.at[lo, g, zo], xbuf.at[g, zo], cs, cr.at[g, zo], dev(core=1 - core)).start()

    def piece(dz, half):
        zz = zplus(dz)
        return part.at[core, zz // 4, zz % 2, pl.ds(pl.multiple_of((zz // 2) % 2 * 128 + half * 64, 64), 64), :]

    def tr_send(steps, half, upward):
        ss, sr, buf = (us, ur, up) if upward else (ds, dr, down)
        slot = buf.at[steps - 1, half]
        rcopy(piece(steps if upward else 8 - steps, half), slot, ss, sr.at[steps - 1, half],
              dev(z=zplus(1 if upward else 7))).start()

    def tr_add(steps, half, upward):
        sr, buf = (ur, up) if upward else (dr, down)
        got(buf.at[steps, half], sr.at[steps, half])
        mine = piece(steps if upward else (8 - steps) % 8, half)
        mine[...] += buf[steps, half]

    def tr_start(lo):
        @pl.when(core == lo)
        def _():
            for g in range(2):
                for zo in range(2):
                    got(xbuf.at[g, zo], cr.at[g, zo])
                    part[core, g, zo] += xbuf[g, zo]
            tr_send(4, 0, True)
            tr_send(4, 1, False)
            tr_send(3, 1, True)
            tr_send(3, 0, False)

    def tr_step(lo, steps):
        @pl.when(core == lo)
        def _():
            tr_add(steps, 0, True)
            tr_send(steps, 0, True)
            tr_add(steps, 1, False)
            tr_send(steps, 1, False)
            if steps > 1:
                tr_add(steps - 1, 1, True)
                tr_send(steps - 1, 1, True)
                tr_add(steps - 1, 0, False)
                tr_send(steps - 1, 0, False)

    def tr_end(lo):
        @pl.when(core == lo)
        def _():
            zo, base = zlo, (z // 2) % 2 * 128
            for half in (1, 0):
                got(up.at[0, half], ur.at[0, half])
                got(down.at[0, 1 - half], dr.at[0, 1 - half])
            for half in range(2):
                mine = part[core, z // 4, zo, pl.ds(pl.multiple_of(base + half * 64, 64), 64), :]
                o_ref[half * 64:(half + 1) * 64, :] = mine + up[0, half] + down[0, half]

    def drain():
        left(Sc.at[0, 0:480], a_s)
        left(S.at[0], ys)
        left(Sc.at[0, 0:512], fs)

        @pl.when(is_src)
        def _():
            left(S, xs)

        @pl.when(is_mid)
        def _():
            left(S.at[0], gs)

        for c in sends:
            c.wait_send()
        left(xbuf, cs)
        left(Sc.at[0, 0:448], us)
        left(Sc.at[0, 0:448], ds)

    a_wait(0)
    y_own(0)
    x_send(0, (0,))
    tr_weights()
    a_wait(1)
    y_own(1)
    x_send(1, (0,))
    y_wait(0)
    x_send(0, (1, 2))
    a_wait(2)
    y_own(2)
    x_send(2, (0,))
    y_wait(1)
    x_send(1, (1, 2))
    a_wait(3)
    y_own(3)
    psum_own(0)
    x_send(3, (0,))
    y_last(0)
    x_send(0, (3,))
    x_local(0)
    y_wait(2)
    x_send(2, (1, 2))
    a_wait(4)
    y_own(4)
    x_send(4, (0,))
    y_last(1)
    x_send(1, (3,))
    x_local(1)
    psum_x(0)
    y_wait(3)
    x_send(3, (1, 2))
    a_wait(5)
    y_own(5)
    x_fwd(0)
    y_last(2)
    x_send(2, (3,))
    x_local(2)
    y_wait(4)
    x_send(4, (1, 2))
    a_wait(6)
    y_own(6)
    x_send(5, (0,))
    psum_y(0)
    y_last(3)
    x_send(3, (3,))
    x_local(3)
    a_wait(7)
    psum_own(1)
    x_fwd(1)
    scale_s(0)
    y_wait(5)
    x_send(5, (1, 2))
    y_own(7)
    y_last(4)
    x_send(4, (3,))
    x_local(4)
    x_last(0)
    multiply(0)
    x_fwd(2)
    y_wait(6)
    y_last(5)
    x_send(5, (3,))
    x_local(5)
    x_last(1)
    multiply(1)
    psum_x(1)
    y_wait(7)
    y_last(6)
    x_rest(6)
    x_local(6)
    x_fwd(3)
    x_last(2)
    multiply(2)
    y_last(7)
    x_rest(7)
    x_local(7)
    x_fwd(4)
    psum_y(1)
    scale_s(1)
    x_fwd(5)
    x_last(3)
    multiply(3)
    x_last(4)
    multiply(4)
    x_fwd(6)
    x_last(5)
    multiply(5)
    tr_start(0)
    x_fwd(7)
    x_last(6)
    multiply(6)
    tr_step(0, 3)
    x_last(7)
    multiply(7)
    tr_step(0, 2)
    tr_start(1)
    tr_step(0, 1)
    tr_step(1, 3)
    tr_step(1, 2)
    tr_step(1, 1)
    tr_end(0)
    tr_end(1)
    drain()


def solution(mesh):
    def on_device(snapshots, cell_weights):
        per_device, cells = snapshots.shape
        snaps = per_device * mesh.shape["row"] * mesh.shape["col"]
        width = cells // 16 // PARTS
        dma, bf16, f32 = pltpu.SemaphoreType.DMA, jnp.bfloat16, jnp.float32
        V = pltpu.VMEM
        return pl.pallas_call(
            functools.partial(kernel, snaps, cells),
            out_shape=jax.ShapeDtypeStruct((128, 512), f32),
            in_specs=[pl.BlockSpec(memory_space=pl.ANY), pl.BlockSpec(memory_space=pl.ANY)],
            out_specs=pl.BlockSpec(memory_space=V),
            scratch_shapes=[
                V((PARTS, 2, 2, 2, 4, 32, width), bf16),
                V((PARTS, 2, 2, 2, 4, 32, width), bf16),
                V((PARTS, 1024, width), bf16),
                V((256, width), bf16),
                V((2, 2, 2, 256, 512), f32),
                V((2, 2, 256, 512), f32),
                V((4, 2, 64, 512), f32),
                V((4, 2, 64, 512), f32),
                V((PARTS, 4, 1, width), f32),
                V((PARTS, 4, 1, width), f32),
                V((PARTS, 1, width), f32),
                V((PARTS, 1, width), f32),
                V((cells // 128, 128), f32),
                dma, dma((PARTS, 4)),
                dma, dma((ROUNDS, 2)), dma, dma((ROUNDS,)),
                dma, dma((ROUNDS, 4, 2)), dma, dma((ROUNDS,)),
                dma((PARTS, 3)), dma((PARTS, 3)), dma((PARTS, 3)), dma((PARTS, 3)),
                dma, dma((2, 2)), dma, dma((4, 2)), dma, dma((4, 2)), dma((ROUNDS,)), dma,
            ],
            compiler_params=pltpu.CompilerParams(
                collective_id=0, has_side_effects=True, vmem_limit_bytes=60 * 1024 * 1024),
        )(snapshots, cell_weights.reshape(cells // 128, 128))

    return jax.shard_map(
        on_device,
        mesh=mesh,
        in_specs=(P(("row", "col"), None), P()),
        out_specs=P("col", "row"),
        check_vma=False,
    )
```

```python
import functools

import jax
import jax.numpy as jnp
from jax import lax
from jax.experimental import pallas as pl
from jax.experimental.pallas import tpu as pltpu
from jax.sharding import PartitionSpec as P

MESH = pl.DeviceIdType.MESH
YOFF = (0, 3, 1, 2)
PARTS = 2
FIRST = 1024
ROUNDS = 4 * PARTS


def kernel(snaps, cells, x_ref, w_hbm, o_ref, S, R, Sc, Rc, psx, psy, mean, fac, part, xbuf, up, down, w_ref,
           a_s, a_r, ys, yr, fs, fr, xs, xr, gs, gr, pxs, pxr, pys, pyr, cs, cr, us, ur, ds, dr, ls, ws):
    slab = cells // 16
    widths = (FIRST, slab - FIRST)
    row, col = lax.axis_index("row"), lax.axis_index("col")
    zlo, x = row // 4, row % 4
    zhi, y, core = col // 8, (col // 2) % 4, col % 2
    z = zhi * 2 + zlo
    is_src = (x % 2) == (y // 2)
    is_mid = jnp.logical_not(is_src)

    def dev(z=z, x=x, y=y, core=core):
        return ((z % 2) * 4 + x, (z // 2) * 8 + y * 2 + core)

    def xplus(d):
        return (x + d) % 4

    def yplus(d):
        return (y + d) % 4

    def zplus(d):
        return (z + d) % 8

    def side(d):
        return 1 if d == 0 else 3

    def rcopy(src, dst, ssem, rsem, device):
        return pltpu.make_async_remote_copy(src_ref=src, dst_ref=dst, send_sem=ssem, recv_sem=rsem,
                                            device_id=device, device_id_type=MESH)

    def got(ref, rsem):
        rcopy(ref, ref, a_s.at[0], rsem, dev(core=1 - core)).wait_recv()

    def left(ref, ssem):
        rcopy(ref, ref, ssem, a_r.at[0, 0], dev(core=1 - core)).wait_send()

    sends = []

    weights = pltpu.make_async_copy(w_hbm, w_ref, ws)
    weights.start()

    barrier = pltpu.get_barrier_semaphore()
    peers = [dev(y=yplus(d)) for d in (1, 2, 3)] + [dev(x=xplus(d)) for d in (1, 2, 3)]
    for dz in range(8):
        for dc in range(2):
            if dz or dc:
                peers.append(dev(z=zplus(dz), core=(core + dc) % 2))

    def barrier_all():
        for peer in peers:
            pl.semaphore_signal(barrier, inc=1, device_id=peer, device_id_type=MESH)
        pl.semaphore_wait(barrier, len(peers))

    barrier_all()

    def order(w):
        part_of, v = w // 4, w % 4
        m = (z + (2, 0, 1, 3)[v]) % 4 if part_of < PARTS - 1 else v
        return part_of, m % 2, m // 2

    me_slot = z * 2 + core

    def tr_cells(k):
        block = S[k].at[zlo, zhi // 2, zhi % 2, y, pl.ds(pl.multiple_of(core * 16, 16), 16), :]
        for dz in (6, 2, 0, 4, 7, 3, 1, 5):
            for dc in range(2):
                z_t, core_t = zplus(dz), (core + dc) % 2
                first = (z_t * 2 + core_t) * slab + k * FIRST
                src = x_ref.at[:, pl.ds(pl.multiple_of(first, 128), widths[k])]
                if dz == 0 and dc == 0:
                    pltpu.make_async_copy(src, block, a_r.at[k, z % 4]).start()
                else:
                    rcopy(src, block, a_s.at[k], a_r.at[k, z % 4], dev(z=z_t, core=core_t)).start()

    late = z % 4 >= 2

    def tr_cells_late():
        @pl.when(late)
        def _():
            tr_cells(1)

    tr_cells(0)

    @pl.when(jnp.logical_not(late))
    def _():
        tr_cells(1)

    def tr_weights():
        weights.wait()
        total = jnp.sum(w_ref[...])
        scale = jnp.sqrt(w_ref[pl.ds(pl.multiple_of(me_slot * 16, 16), 16), :] / total)
        for j in range(16):
            k, at = (0, j * 128) if j * 128 < FIRST else (1, j * 128 - FIRST)
            fac[k][:, at:at + 128] = scale[j:j + 1, :]

    def a_wait(w):
        k, g, lo = order(w)
        got(S[k].at[g, :, lo, y], a_r.at[k, 2 * lo + g])

    def y_own(w):
        k, g, lo = order(w)
        unit = S[k].at[g, :, lo, y]
        for d in range(2):
            rcopy(unit, unit, ys.at[k], yr.at[w, d], dev(y=yplus(side(d)))).start()

    def y_wait(w):
        k, g, lo = order(w)
        for d in range(2):
            yy = yplus(4 - side(d))
            got(S[k].at[g, :, lo, yy], yr.at[w, d])
            half = S[k].at[g, d, lo, yy]
            rcopy(half, half, fs.at[k], fr.at[w], dev(y=yplus(side(d)))).start()

    def y_last(w):
        k, g, lo = order(w)
        got(S[k].at[g, :, lo, yplus(2)], fr.at[w])

    def x_send(w, js):
        k, g, lo = order(w)

        @pl.when(is_src)
        def _():
            for j in js:
                yy = yplus(YOFF[j])
                for d in range(2):
                    rcopy(S[k].at[g, y % 2, lo, yy], R[k].at[g, x // 2, lo, yy],
                          xs.at[k], xr.at[w, j, d], dev(x=xplus(side(d)))).start()

    def x_rest(w):
        k, g, lo = order(w)

        @pl.when(is_src)
        def _():
            for pos in range(4):
                for d in range(2):
                    j = ((0, 2, 1, 3), (1, 3, 0, 2))[d][pos]
                    yy = yplus(YOFF[j])
                    rcopy(S[k].at[g, y % 2, lo, yy], R[k].at[g, x // 2, lo, yy],
                          xs.at[k], xr.at[w, j, d], dev(x=xplus(side(d)))).start()

    def x_local(w):
        k, g, lo = order(w)

        @pl.when(is_src)
        def _():
            pltpu.make_async_copy(S[k].at[g, y % 2, lo], R[k].at[g, x // 2, lo], ls.at[w]).start()

    def x_fwd(w):
        k, g, lo = order(w)

        @pl.when(is_mid)
        def _():
            for n in range(8):
                if w < 6:
                    j, d = n // 2, (n // 2 + n) % 2
                else:
                    d = n % 2
                    j = ((0, 2, 1, 3), (1, 3, 0, 2))[d][n // 2]
                yy = yplus(YOFF[j])
                if True:
                    unit = R[k].at[g, xplus(4 - side(d)) // 2, lo, yy]
                    got(unit, xr.at[w, j, d])
                    if j % 2 == d:
                        rcopy(unit, unit, gs.at[k], gr.at[w], dev(x=xplus(side(d)))).start()

    def x_last(w):
        k, g, lo = order(w)

        @pl.when(is_src)
        def _():
            got(R[k].at[g, 1 - x // 2, lo], gr.at[w])
            own = R[k].at[g, x // 2, lo]
            pltpu.make_async_copy(own, own, ls.at[w]).wait()

    def psum_own(k):
        def body(i, carry):
            block = S[k][i // 4, (i // 2) % 2, i % 2, y].astype(jnp.float32)
            return carry + (block[0:8] + block[8:16]) + (block[16:24] + block[24:32])

        total8 = lax.fori_loop(0, 8, body, jnp.zeros((8, widths[k]), jnp.float32))
        psx[k][x] = jnp.sum(total8, axis=0, keepdims=True)
        for d in (1, 2, 3):
            c = rcopy(psx[k].at[x], psx[k].at[x], pxs.at[k, d - 1], pxr.at[k, d - 1], dev(x=xplus(d)))
            c.start()
            sends.append(c)

    def psum_x(k):
        for d in (1, 2, 3):
            got(psx[k].at[xplus(4 - d)], pxr.at[k, d - 1])
        psy[k][y] = (psx[k][0] + psx[k][1]) + (psx[k][2] + psx[k][3])
        for d in (1, 2, 3):
            c = rcopy(psy[k].at[y], psy[k].at[y], pys.at[k, d - 1], pyr.at[k, d - 1], dev(y=yplus(d)))
            c.start()
            sends.append(c)

    def psum_y(k):
        for d in (1, 2, 3):
            got(psy[k].at[yplus(4 - d)], pyr.at[k, d - 1])
        mean[k][...] = ((psy[k][0] + psy[k][1]) + (psy[k][2] + psy[k][3])) / snaps

    def scaled(k, block):
        return ((block.astype(jnp.float32) - mean[k][...]) * fac[k][...]).astype(jnp.bfloat16)

    def scale_s(w):
        k, g, lo = order(w)

        def body(i, carry):
            at = g * 512 + (i // 4) * 256 + lo * 128 + (i % 4) * 32
            Sc[k][pl.ds(pl.multiple_of(at, 32), 32), :] = scaled(k, S[k][g, i // 4, lo, i % 4])
            return carry

        lax.fori_loop(0, 8, body, 0)

    def multiply(w):
        k, g, lo = order(w)

        def body(i, carry):
            Rc[k][pl.ds(pl.multiple_of(i * 32, 32), 32), :] = scaled(k, R[k][g, i // 4, lo, i % 4])
            return carry

        lax.fori_loop(0, 8, body, 0)

        def dot(zo, carry):
            product = lax.dot_general(
                Rc[k][...], Sc[k][pl.ds(zo * 512 if isinstance(zo, int) else pl.multiple_of(zo * 512, 512), 512), :],
                (((1,), (1,)), ((), ())), preferred_element_type=jnp.float32)
            if k == 0:
                part[lo, g, zo] = product
            else:
                part[lo, g, zo] += product
            return carry

        if k == 0:
            lax.fori_loop(0, 2, dot, 0)
        else:
            for zo in range(2):
                dot(zo, 0)
                give(lo, g, zo)

    def give(lo, g, zo):
        @pl.when(core == 1 - lo)
        def _():
            rcopy(part.at[lo, g, zo], xbuf.at[g, zo], cs, cr.at[g, zo], dev(core=1 - core)).start()

    def piece(dz, half):
        zz = zplus(dz)
        return part.at[core, zz // 4, zz % 2, pl.ds(pl.multiple_of((zz // 2) % 2 * 128 + half * 64, 64), 64), :]

    def tr_send(steps, half, upward):
        ss, sr, buf = (us, ur, up) if upward else (ds, dr, down)
        slot = buf.at[2 * steps - 2 + half]
        rcopy(piece(steps if upward else 8 - steps, half), slot, ss, sr.at[steps - 1, half],
              dev(z=zplus(1 if upward else 7))).start()

    def tr_add(steps, half, upward):
        sr, buf = (ur, up) if upward else (dr, down)
        got(buf.at[2 * steps + half], sr.at[steps, half])
        mine = piece(steps if upward else (8 - steps) % 8, half)
        mine[...] += buf[2 * steps + half]

    def tr_start(lo):
        @pl.when(core == lo)
        def _():
            for g in range(2):
                for zo in range(2):
                    got(xbuf.at[g, zo], cr.at[g, zo])
                    part[core, g, zo] += xbuf[g, zo]
            tr_send(4, 0, True)
            tr_send(4, 1, False)
            tr_send(3, 1, True)
            tr_send(3, 0, False)

    def tr_step(lo, steps):
        @pl.when(core == lo)
        def _():
            tr_add(steps, 0, True)
            tr_send(steps, 0, True)
            tr_add(steps, 1, False)
            tr_send(steps, 1, False)
            if steps > 1:
                tr_add(steps - 1, 1, True)
                tr_send(steps - 1, 1, True)
                tr_add(steps - 1, 0, False)
                tr_send(steps - 1, 0, False)

    def tr_end(lo):
        @pl.when(core == lo)
        def _():
            zo, base = zlo, (z // 2) % 2 * 128
            for half in (1, 0):
                got(up.at[half], ur.at[0, half])
                got(down.at[1 - half], dr.at[0, 1 - half])
            for half in range(2):
                mine = part[core, z // 4, zo, pl.ds(pl.multiple_of(base + half * 64, 64), 64), :]
                o_ref[half * 64:(half + 1) * 64, :] = mine + up[half] + down[half]

    def drain():
        for k in range(PARTS):
            left(Sc[k].at[0:240], a_s.at[k])
            left(S[k].at[0], ys.at[k])
            left(S[k].at[0, 0], fs.at[k])

            @pl.when(is_src)
            def _(k=k):
                left(S[k], xs.at[k])

            @pl.when(is_mid)
            def _(k=k):
                left(S[k].at[0], gs.at[k])

        for c in sends:
            c.wait_send()
        left(xbuf, cs)
        left(up.at[0:7], us)
        left(up.at[0:7], ds)

    a_wait(0)
    y_own(0)
    x_send(0, (0,))
    tr_weights()
    a_wait(1)
    y_own(1)
    x_send(1, (0,))
    y_wait(0)
    x_send(0, (1, 2))
    a_wait(2)
    y_own(2)
    x_send(2, (0,))
    y_wait(1)
    x_send(1, (1, 2))
    a_wait(3)
    tr_cells_late()
    y_own(3)
    psum_own(0)
    x_send(3, (0,))
    y_last(0)
    x_send(0, (3,))
    x_local(0)
    y_wait(2)
    x_send(2, (1, 2))
    a_wait(4)
    y_own(4)
    x_send(4, (0,))
    y_last(1)
    x_send(1, (3,))
    x_local(1)
    psum_x(0)
    y_wait(3)
    x_send(3, (1, 2))
    a_wait(5)
    y_own(5)
    x_fwd(0)
    y_last(2)
    x_send(2, (3,))
    x_local(2)
    y_wait(4)
    x_send(4, (1, 2))
    a_wait(6)
    y_own(6)
    x_send(5, (0,))
    psum_y(0)
    y_last(3)
    x_send(3, (3,))
    x_local(3)
    a_wait(7)
    psum_own(1)
    x_fwd(1)
    y_wait(5)
    x_send(5, (1, 2))
    y_own(7)
    scale_s(0)
    scale_s(1)
    scale_s(2)
    scale_s(3)
    y_last(4)
    x_send(4, (3,))
    x_local(4)
    x_fwd(2)
    x_last(0)
    multiply(0)
    y_wait(6)
    y_last(5)
    x_send(5, (3,))
    x_local(5)
    x_fwd(3)
    x_last(1)
    multiply(1)
    psum_x(1)
    y_wait(7)
    y_last(6)
    x_rest(6)
    x_local(6)
    x_last(2)
    multiply(2)
    x_fwd(4)
    psum_y(1)
    scale_s(4)
    scale_s(5)
    scale_s(6)
    y_last(7)
    x_rest(7)
    x_local(7)
    x_fwd(5)
    scale_s(7)
    x_last(3)
    multiply(3)
    x_last(4)
    multiply(4)
    x_last(5)
    multiply(5)
    x_fwd(6)
    tr_start(0)
    x_fwd(7)
    x_last(6)
    multiply(6)
    x_last(7)
    multiply(7)
    tr_step(0, 3)
    tr_start(1)
    tr_step(0, 2)
    tr_step(0, 1)
    tr_step(1, 3)
    tr_step(1, 2)
    tr_step(1, 1)
    tr_end(0)
    tr_end(1)
    drain()


def solution(mesh):
    def on_device(snapshots, cell_weights):
        per_device, cells = snapshots.shape
        snaps = per_device * mesh.shape["row"] * mesh.shape["col"]
        widths = (FIRST, cells // 16 - FIRST)
        dma, bf16, f32 = pltpu.SemaphoreType.DMA, jnp.bfloat16, jnp.float32
        V = pltpu.VMEM
        return pl.pallas_call(
            functools.partial(kernel, snaps, cells),
            out_shape=jax.ShapeDtypeStruct((128, 512), f32),
            in_specs=[pl.BlockSpec(memory_space=pl.ANY), pl.BlockSpec(memory_space=pl.ANY)],
            out_specs=pl.BlockSpec(memory_space=V),
            scratch_shapes=[
                [V((2, 2, 2, 4, 32, n), bf16) for n in widths],
                [V((2, 2, 2, 4, 32, n), bf16) for n in widths],
                [V((1024, n), bf16) for n in widths],
                [V((256, n), bf16) for n in widths],
                [V((4, 1, n), f32) for n in widths],
                [V((4, 1, n), f32) for n in widths],
                [V((1, n), f32) for n in widths],
                [V((1, n), f32) for n in widths],
                V((2, 2, 2, 256, 512), f32),
                V((2, 2, 256, 512), f32),
                V((8, 64, 512), f32),
                V((8, 64, 512), f32),
                V((cells // 128, 128), f32),
                dma((PARTS,)), dma((PARTS, 4)),
                dma((PARTS,)), dma((ROUNDS, 2)), dma((PARTS,)), dma((ROUNDS,)),
                dma((PARTS,)), dma((ROUNDS, 4, 2)), dma((PARTS,)), dma((ROUNDS,)),
                dma((PARTS, 3)), dma((PARTS, 3)), dma((PARTS, 3)), dma((PARTS, 3)),
                dma, dma((2, 2)), dma, dma((4, 2)), dma, dma((4, 2)), dma((ROUNDS,)), dma,
            ],
            compiler_params=pltpu.CompilerParams(
                collective_id=0, has_side_effects=True, vmem_limit_bytes=60 * 1024 * 1024),
        )(snapshots, cell_weights.reshape(cells // 128, 128))

    return jax.shard_map(
        on_device,
        mesh=mesh,
        in_specs=(P(("row", "col"), None), P()),
        out_specs=P("col", "row"),
        check_vma=False,
    )
```

```python
import functools

import jax
import jax.numpy as jnp
from jax import lax
from jax.experimental import pallas as pl
from jax.experimental.pallas import tpu as pltpu
from jax.sharding import PartitionSpec as P

MESH = pl.DeviceIdType.MESH
YOFF = (0, 3, 1, 2)
PARTS = 2
FIRST = 1024
SUBS = (2, 2)
ROUNDS = 4 * PARTS


def kernel(snaps, cells, x_ref, w_hbm, o_ref, S, R, Sc, Rc, psx, psy, mean, fac, part, xbuf, up, down, eup, edown, obuf, w_ref,
           a_s, a_r, ys, yr, fs, fr, xs, xr, gs, gr, pxs, pxr, pys, pyr, cs, cr, us, ur, ds, dr, eur, edr, os, orr, ls, ws):
    slab = cells // 16
    widths = (FIRST, slab - FIRST)
    row, col = lax.axis_index("row"), lax.axis_index("col")
    zlo, x = row // 4, row % 4
    zhi, y, core = col // 8, (col // 2) % 4, col % 2
    z = zhi * 2 + zlo
    is_src = (x % 2) == (y // 2)
    is_mid = jnp.logical_not(is_src)

    def dev(z=z, x=x, y=y, core=core):
        return ((z % 2) * 4 + x, (z // 2) * 8 + y * 2 + core)

    def xplus(d):
        return (x + d) % 4

    def yplus(d):
        return (y + d) % 4

    def zplus(d):
        return (z + d) % 8

    def side(d):
        return 1 if d == 0 else 3

    def rcopy(src, dst, ssem, rsem, device):
        return pltpu.make_async_remote_copy(src_ref=src, dst_ref=dst, send_sem=ssem, recv_sem=rsem,
                                            device_id=device, device_id_type=MESH)

    def got(ref, rsem):
        rcopy(ref, ref, a_s.at[0], rsem, dev(core=1 - core)).wait_recv()

    def left(ref, ssem):
        rcopy(ref, ref, ssem, a_r.at[0, 0], dev(core=1 - core)).wait_send()


    weights = pltpu.make_async_copy(w_hbm, w_ref, ws)
    weights.start()

    barrier = pltpu.get_barrier_semaphore()
    peers = [dev(y=yplus(d)) for d in (1, 2, 3)] + [dev(x=xplus(d)) for d in (1, 2, 3)]
    for dz in range(8):
        for dc in range(2):
            if dz or dc:
                peers.append(dev(z=zplus(dz), core=(core + dc) % 2))

    def barrier_all():
        for peer in peers:
            pl.semaphore_signal(barrier, inc=1, device_id=peer, device_id_type=MESH)
        pl.semaphore_wait(barrier, len(peers))

    barrier_all()

    late_lo = (z + 1) // 2 % 2

    def order(w):
        part_of, v = w // 4, w % 4
        m = (z + (2, 0, 1 + 2 * late_lo, 3 - 2 * late_lo)[v]) % 4 if part_of < PARTS - 1 else v
        return part_of, m % 2, m // 2

    me_slot = z * 2 + core

    def tr_cells(k):
        block = S[k].at[zlo, zhi // 2, zhi % 2, y, pl.ds(pl.multiple_of(core * 16, 16), 16), :]
        for dz in (6, 2, 0, 4, 7, 3, 1, 5):
            for dc in range(2):
                z_t, core_t = zplus(dz), (core + dc) % 2
                first = (z_t * 2 + core_t) * slab + k * FIRST
                src = x_ref.at[:, pl.ds(pl.multiple_of(first, 128), widths[k])]
                if dz == 0 and dc == 0:
                    pltpu.make_async_copy(src, block, a_r.at[k, z % 4]).start()
                else:
                    rcopy(src, block, a_s.at[k], a_r.at[k, z % 4], dev(z=z_t, core=core_t)).start()

    late = z % 4 >= 2

    def tr_cells_late():
        @pl.when(late)
        def _():
            tr_cells(1)

    tr_cells(0)

    @pl.when(jnp.logical_not(late))
    def _():
        tr_cells(1)

    def tr_weights():
        weights.wait()
        total = jnp.sum(w_ref[...])
        scale = jnp.sqrt(w_ref[pl.ds(pl.multiple_of(me_slot * 16, 16), 16), :] / total)
        for j in range(16):
            k, at = (0, j * 128) if j * 128 < FIRST else (1, j * 128 - FIRST)
            fac[k][:, at:at + 128] = scale[j:j + 1, :]

    def a_wait(w):
        k, g, lo = order(w)
        got(S[k].at[g, :, lo, y], a_r.at[k, 2 * lo + g])

    def y_own(w):
        k, g, lo = order(w)
        unit = S[k].at[g, :, lo, y]
        for d in range(2):
            rcopy(unit, unit, ys.at[k], yr.at[w, d], dev(y=yplus(side(d)))).start()

    def y_wait(w):
        k, g, lo = order(w)
        for d in range(2):
            yy = yplus(4 - side(d))
            got(S[k].at[g, :, lo, yy], yr.at[w, d])
            half = S[k].at[g, d, lo, yy]
            rcopy(half, half, fs.at[k], fr.at[w], dev(y=yplus(side(d)))).start()

    def y_last(w):
        k, g, lo = order(w)
        got(S[k].at[g, :, lo, yplus(2)], fr.at[w])

    def x_send(w, js):
        k, g, lo = order(w)

        @pl.when(is_src)
        def _():
            for j in js:
                yy = yplus(YOFF[j])
                for d in range(2):
                    rcopy(S[k].at[g, y % 2, lo, yy], R[k].at[g, x // 2, lo, yy],
                          xs.at[k], xr.at[w, j if j % 2 == d else 4], dev(x=xplus(side(d)))).start()

    def x_rest(w):
        k, g, lo = order(w)

        @pl.when(is_src)
        def _():
            for pos in range(4):
                for d in range(2):
                    j = ((0, 2, 1, 3), (1, 3, 0, 2))[d][pos]
                    yy = yplus(YOFF[j])
                    rcopy(S[k].at[g, y % 2, lo, yy], R[k].at[g, x // 2, lo, yy],
                          xs.at[k], xr.at[w, j if j % 2 == d else 4], dev(x=xplus(side(d)))).start()

    def x_local(w):
        k, g, lo = order(w)

        @pl.when(is_src)
        def _():
            pltpu.make_async_copy(S[k].at[g, y % 2, lo], R[k].at[g, x // 2, lo], ls.at[w]).start()

    def x_fwd(w):
        k, g, lo = order(w)

        @pl.when(is_mid)
        def _():
            for n in range(8):
                if w not in (6, 7):
                    j, d = n // 2, (n // 2 + n) % 2
                else:
                    d = n % 2
                    j = ((0, 2, 1, 3), (1, 3, 0, 2))[d][n // 2]
                yy = yplus(YOFF[j])
                if True:
                    unit = R[k].at[g, xplus(4 - side(d)) // 2, lo, yy]
                    if j % 2 == d:
                        got(unit, xr.at[w, j])
                        rcopy(unit, unit, gs.at[k], gr.at[w], dev(x=xplus(side(d)))).start()

    def x_last(w):
        k, g, lo = order(w)

        @pl.when(is_src)
        def _():
            got(R[k].at[g, 1 - x // 2, lo], gr.at[w])
            own = R[k].at[g, x // 2, lo]
            pltpu.make_async_copy(own, own, ls.at[w]).wait()

        @pl.when(is_mid)
        def _():
            got(R[k].at[g, 0, lo], xr.at[w, 4])

    def psum_own(k):
        def body(i, carry):
            block = S[k][i // 4, (i // 2) % 2, i % 2, y].astype(jnp.float32)
            return carry + (block[0:8] + block[8:16]) + (block[16:24] + block[24:32])

        total8 = lax.fori_loop(0, 8, body, jnp.zeros((8, widths[k]), jnp.float32))
        psx[k][x] = jnp.sum(total8, axis=0, keepdims=True)
        for d in (1, 2, 3):
            c = rcopy(psx[k].at[x], psx[k].at[x], pxs.at[k], pxr.at[k], dev(x=xplus(d)))
            c.start()

    def psum_x(k):
        got(psx[k].at[0:3], pxr.at[k])
        psy[k][y] = (psx[k][0] + psx[k][1]) + (psx[k][2] + psx[k][3])
        for d in (1, 2, 3):
            c = rcopy(psy[k].at[y], psy[k].at[y], pys.at[k], pyr.at[k], dev(y=yplus(d)))
            c.start()

    def psum_y(k):
        got(psy[k].at[0:3], pyr.at[k])
        mean[k][...] = ((psy[k][0] + psy[k][1]) + (psy[k][2] + psy[k][3])) / snaps

    def scaled(k, block):
        return ((block.astype(jnp.float32) - mean[k][...]) * fac[k][...]).astype(jnp.bfloat16)

    def scale_s(w):
        k, g, lo = order(w)

        def body(i, carry):
            at = g * 512 + (i // 4) * 256 + lo * 128 + (i % 4) * 32
            Sc[k][pl.ds(pl.multiple_of(at, 32), 32), :] = scaled(k, S[k][g, i // 4, lo, i % 4])
            return carry

        lax.fori_loop(0, 8, body, 0)

    def multiply(w):
        k, g, lo = order(w)

        def body(i, carry):
            Rc[k][pl.ds(pl.multiple_of(i * 32, 32), 32), :] = scaled(k, R[k][g, i // 4, lo, i % 4])
            return carry

        lax.fori_loop(0, 8, body, 0)

        def dot(zo, carry):
            product = lax.dot_general(
                Rc[k][...], Sc[k][pl.ds(zo * 512 if isinstance(zo, int) else pl.multiple_of(zo * 512, 512), 512), :],
                (((1,), (1,)), ((), ())), preferred_element_type=jnp.float32)
            if k == 0:
                part[lo, g, zo] = product.reshape(2, 2, 64, 512)
            else:
                part[lo, g, zo] += product.reshape(2, 2, 64, 512)
            return carry

        if k == 0:
            lax.fori_loop(0, 2, dot, 0)
        else:
            for zo in range(2):
                dot(zo, 0)
                give(lo, g, zo)

    def give(lo, g, zo):
        rcopy(part.at[lo, g, zo, :, 1 - core], xbuf.at[lo, g, zo], cs, cr.at[lo, g, zo], dev(core=1 - core)).start()

    def piece(lo, dz, half, sub):
        zz, rows = zplus(dz), 32 // SUBS[lo]
        return part.at[lo, zz // 4, zz % 2, (zz // 2) % 2, core, pl.ds(half * 32 + sub * rows, rows), :]

    def tr_send(lo, steps, half, sub, upward):
        ss, sr, buf, fr_, fb = (us, ur, up, eur, eup) if upward else (ds, dr, down, edr, edown)
        src, z_t = piece(lo, steps if upward else 8 - steps, half, sub), zplus(1 if upward else 7)
        if steps > 1:
            slot = ((steps - 2) * 2 + half) * SUBS[lo] + sub
            rcopy(src, buf[lo].at[slot], ss, sr[lo].at[slot], dev(z=z_t)).start()
        else:
            rows, n = 32 // SUBS[lo], half * SUBS[lo] + sub
            rcopy(src, fb.at[core, pl.ds(half * 32 + sub * rows, rows), :], ss, fr_.at[core, n], dev(z=z_t, core=lo)).start()

    def tr_pass(lo, steps, half, upward):
        sr, buf = (ur, up) if upward else (dr, down)

        def one(sub):
            slot = ((steps - 1) * 2 + half) * SUBS[lo] + sub
            got(buf[lo].at[slot], sr[lo].at[slot])
            mine = piece(lo, steps if upward else 8 - steps, half, sub)
            mine[...] += buf[lo][slot]
            tr_send(lo, steps, half, sub, upward)

        return one

    def tr_start(lo):
        for g in range(2):
            for zo in range(2):
                got(xbuf.at[lo, g, zo], cr.at[lo, g, zo])
                part[lo, g, zo, :, core] += xbuf[lo, g, zo]
        for steps, half in ((4, 0), (3, 1)):
            for sub in range(SUBS[lo]):
                tr_send(lo, steps, half, sub, True)
                tr_send(lo, steps, 1 - half, sub, False)

        @pl.when(core != lo)
        def _():
            rcopy(part.at[lo, z // 4, zlo, (z // 2) % 2, core], obuf, os, orr, dev(core=1 - core)).start()

    def tr_step(lo, steps):
        for st, half in ((steps, 0), (steps - 1, 1)):
            if st > 0:
                for sub in range(SUBS[lo]):
                    tr_pass(lo, st, half, True)(sub)
                    tr_pass(lo, st, 1 - half, False)(sub)

    def tr_end(lo):
        @pl.when(core == lo)
        def _():
            got(obuf, orr)
            for c in range(2):
                for n in range(2 * SUBS[lo]):
                    rows = 32 // SUBS[lo]
                    got(eup.at[c, n * rows:(n + 1) * rows, :], eur.at[c, n])
                    got(edown.at[c, n * rows:(n + 1) * rows, :], edr.at[c, n])
            mine = part[lo, z // 4, zlo, (z // 2) % 2, lo]
            o_ref[lo * 64:(lo + 1) * 64, :] = mine + eup[lo] + edown[lo]
            o_ref[(1 - lo) * 64:(2 - lo) * 64, :] = obuf[...] + eup[1 - lo] + edown[1 - lo]

    def drain():
        for k in range(PARTS):
            left(Sc[k].at[0:240], a_s.at[k])
            left(S[k].at[0], ys.at[k])
            left(S[k].at[0, 0], fs.at[k])
            left(psx[k].at[0:3], pxs.at[k])
            left(psy[k].at[0:3], pys.at[k])

            @pl.when(is_src)
            def _(k=k):
                left(S[k], xs.at[k])

            @pl.when(is_mid)
            def _(k=k):
                left(S[k].at[0], gs.at[k])

        left(xbuf, cs)
        left(Sc[0].at[0:448], us)
        left(Sc[0].at[0:448], ds)
        left(obuf, os)

    a_wait(0)
    y_own(0)
    x_send(0, (0,))
    tr_weights()
    a_wait(1)
    y_own(1)
    x_send(1, (0,))
    y_wait(0)
    x_send(0, (1, 2))
    a_wait(2)
    y_own(2)
    x_send(2, (0,))
    y_wait(1)
    x_send(1, (1, 2))
    a_wait(3)
    tr_cells_late()
    y_own(3)
    x_send(3, (0,))
    psum_own(0)
    y_last(0)
    x_send(0, (3,))
    x_local(0)
    y_wait(2)
    x_send(2, (1, 2))
    a_wait(4)
    y_own(4)
    x_send(4, (0,))
    y_last(1)
    x_send(1, (3,))
    x_local(1)
    psum_x(0)
    y_wait(3)
    a_wait(5)
    y_own(5)
    x_fwd(0)
    y_last(2)
    x_send(2, (3,))
    x_local(2)
    y_wait(4)
    x_send(4, (1, 2))
    a_wait(6)
    y_own(6)
    x_send(5, (0,))
    psum_y(0)
    y_last(3)
    x_local(3)
    a_wait(7)
    psum_own(1)
    x_fwd(1)
    y_wait(5)
    x_send(5, (1, 2))
    y_own(7)
    scale_s(0)
    scale_s(1)
    scale_s(2)
    scale_s(3)
    y_last(4)
    x_send(4, (3,))
    x_local(4)
    x_fwd(2)
    x_last(0)
    multiply(0)
    y_wait(6)
    y_last(5)
    x_send(5, (3,))
    x_local(5)
    x_send(3, (1, 2, 3))
    x_last(1)
    multiply(1)
    psum_x(1)
    y_wait(7)
    x_fwd(4)
    y_last(6)
    x_rest(6)
    x_local(6)
    x_last(2)
    multiply(2)
    x_fwd(5)
    psum_y(1)
    scale_s(4)
    scale_s(5)
    scale_s(6)
    y_last(7)
    x_rest(7)
    x_local(7)
    scale_s(7)
    x_last(4)
    multiply(4)
    x_fwd(3)
    x_last(5)
    multiply(5)
    tr_start(0)
    x_last(3)
    multiply(3)
    x_fwd(6)
    tr_step(0, 3)
    x_last(6)
    multiply(6)
    x_fwd(7)
    tr_step(0, 2)
    x_last(7)
    multiply(7)
    tr_step(0, 1)
    tr_start(1)
    tr_step(1, 3)
    tr_step(1, 2)
    tr_step(1, 1)
    tr_end(0)
    tr_end(1)
    drain()


def solution(mesh):
    def on_device(snapshots, cell_weights):
        per_device, cells = snapshots.shape
        snaps = per_device * mesh.shape["row"] * mesh.shape["col"]
        widths = (FIRST, cells // 16 - FIRST)
        dma, bf16, f32 = pltpu.SemaphoreType.DMA, jnp.bfloat16, jnp.float32
        V = pltpu.VMEM
        return pl.pallas_call(
            functools.partial(kernel, snaps, cells),
            out_shape=jax.ShapeDtypeStruct((128, 512), f32),
            in_specs=[pl.BlockSpec(memory_space=pl.ANY), pl.BlockSpec(memory_space=pl.ANY)],
            out_specs=pl.BlockSpec(memory_space=V),
            scratch_shapes=[
                [V((2, 2, 2, 4, 32, n), bf16) for n in widths],
                [V((2, 2, 2, 4, 32, n), bf16) for n in widths],
                [V((1024, n), bf16) for n in widths],
                [V((256, n), bf16) for n in widths],
                [V((4, 1, n), f32) for n in widths],
                [V((4, 1, n), f32) for n in widths],
                [V((1, n), f32) for n in widths],
                [V((1, n), f32) for n in widths],
                V((2, 2, 2, 2, 2, 64, 512), f32),
                V((2, 2, 2, 2, 64, 512), f32),
                [V((6 * n, 32 // n, 512), f32) for n in SUBS],
                [V((6 * n, 32 // n, 512), f32) for n in SUBS],
                V((2, 64, 512), f32),
                V((2, 64, 512), f32),
                V((64, 512), f32),
                V((cells // 128, 128), f32),
                dma((PARTS,)), dma((PARTS, 4)),
                dma((PARTS,)), dma((ROUNDS, 2)), dma((PARTS,)), dma((ROUNDS,)),
                dma((PARTS,)), dma((ROUNDS, 5)), dma((PARTS,)), dma((ROUNDS,)),
                dma((PARTS,)), dma((PARTS,)), dma((PARTS,)), dma((PARTS,)),
                dma, dma((2, 2, 2)), dma, [dma((6 * n,)) for n in SUBS], dma, [dma((6 * n,)) for n in SUBS],
                dma((2, 2 * max(SUBS))), dma((2, 2 * max(SUBS))), dma, dma,
                dma((ROUNDS,)), dma,
            ],
            compiler_params=pltpu.CompilerParams(
                collective_id=0, has_side_effects=True, vmem_limit_bytes=60 * 1024 * 1024),
        )(snapshots, cell_weights.reshape(cells // 128, 128))

    return jax.shard_map(
        on_device,
        mesh=mesh,
        in_specs=(P(("row", "col"), None), P()),
        out_specs=P("col", "row"),
        check_vma=False,
    )
```

```python
import functools

import jax
import jax.numpy as jnp
from jax import lax
from jax.experimental import pallas as pl
from jax.experimental.pallas import tpu as pltpu
from jax.sharding import PartitionSpec as P

MESH = pl.DeviceIdType.MESH
YOFF = (0, 3, 1, 2)
PARTS = 2
FIRST = 1024
SUBS = (2, 2)
ROUNDS = 4 * PARTS


def kernel(snaps, cells, x_ref, w_hbm, o_ref, S, R, Sc, Rc, psx, psy, mean, fac, part, xbuf, up, down, eup, edown, obuf, w_ref,
           a_s, a_r, ys, yr, fs, fr, xs, xr, gs, gr, pxs, pxr, pys, pyr, cs, cr, us, ur, ds, dr, eur, edr, os, orr, ls, ws):
    slab = cells // 16
    widths = (FIRST, slab - FIRST)
    row, col = lax.axis_index("row"), lax.axis_index("col")
    zlo, x = row // 4, row % 4
    zhi, y, core = col // 8, (col // 2) % 4, col % 2
    z = zhi * 2 + zlo
    is_src = (x % 2) == (y // 2)
    is_mid = jnp.logical_not(is_src)

    def dev(z=z, x=x, y=y, core=core):
        return ((z % 2) * 4 + x, (z // 2) * 8 + y * 2 + core)

    def xplus(d):
        return (x + d) % 4

    def yplus(d):
        return (y + d) % 4

    def zplus(d):
        return (z + d) % 8

    def side(d):
        return 1 if d == 0 else 3

    def rcopy(src, dst, ssem, rsem, device):
        return pltpu.make_async_remote_copy(src_ref=src, dst_ref=dst, send_sem=ssem, recv_sem=rsem,
                                            device_id=device, device_id_type=MESH)

    def got(ref, rsem):
        rcopy(ref, ref, a_s.at[0], rsem, dev(core=1 - core)).wait_recv()

    def left(ref, ssem):
        rcopy(ref, ref, ssem, a_r.at[0, 0], dev(core=1 - core)).wait_send()


    weights = pltpu.make_async_copy(w_hbm, w_ref, ws)
    weights.start()

    barrier = pltpu.get_barrier_semaphore()
    peers = [dev(y=yplus(d)) for d in (1, 2, 3)] + [dev(x=xplus(d)) for d in (1, 2, 3)]
    for dz in range(8):
        for dc in range(2):
            if dz or dc:
                peers.append(dev(z=zplus(dz), core=(core + dc) % 2))

    def barrier_all():
        for peer in peers:
            pl.semaphore_signal(barrier, inc=1, device_id=peer, device_id_type=MESH)
        pl.semaphore_wait(barrier, len(peers))

    barrier_all()

    late_lo = (z + 1) // 2 % 2

    def order(w):
        part_of, v = w // 4, w % 4
        m = (z + (2, 0, 1 + 2 * late_lo, 3 - 2 * late_lo)[v]) % 4 if part_of < PARTS - 1 else v
        return part_of, m % 2, m // 2

    me_slot = z * 2 + core

    def tr_cells(k):
        block = S[k].at[zlo, zhi // 2, zhi % 2, y, pl.ds(pl.multiple_of(core * 16, 16), 16), :]
        for dz in (6, 2, 0, 4, 7, 3, 1, 5):
            for dc in range(2):
                z_t, core_t = zplus(dz), (core + dc) % 2
                first = (z_t * 2 + core_t) * slab + k * FIRST
                src = x_ref.at[:, pl.ds(pl.multiple_of(first, 128), widths[k])]
                if dz == 0 and dc == 0:
                    pltpu.make_async_copy(src, block, a_r.at[k, z % 4]).start()
                else:
                    rcopy(src, block, a_s.at[k], a_r.at[k, z % 4], dev(z=z_t, core=core_t)).start()

    late = z % 4 >= 2

    def tr_cells_late():
        @pl.when(late)
        def _():
            tr_cells(1)

    tr_cells(0)

    @pl.when(jnp.logical_not(late))
    def _():
        tr_cells(1)

    def tr_weights():
        weights.wait()
        total = jnp.sum(w_ref[...])
        scale = jnp.sqrt(w_ref[pl.ds(pl.multiple_of(me_slot * 16, 16), 16), :] / total)
        for j in range(16):
            k, at = (0, j * 128) if j * 128 < FIRST else (1, j * 128 - FIRST)
            fac[k][:, at:at + 128] = scale[j:j + 1, :]

    def a_wait(w):
        k, g, lo = order(w)
        got(S[k].at[g, :, lo, y], a_r.at[k, 2 * lo + g])

    def y_own(w):
        k, g, lo = order(w)
        unit = S[k].at[g, :, lo, y]
        for d in range(2):
            rcopy(unit, unit, ys.at[k], yr.at[w, d], dev(y=yplus(side(d)))).start()

    def y_wait(w):
        k, g, lo = order(w)
        for d in range(2):
            yy = yplus(4 - side(d))
            got(S[k].at[g, :, lo, yy], yr.at[w, d])
            half = S[k].at[g, d, lo, yy]
            rcopy(half, half, fs.at[k], fr.at[w], dev(y=yplus(side(d)))).start()

    def y_last(w):
        k, g, lo = order(w)
        got(S[k].at[g, :, lo, yplus(2)], fr.at[w])

    def x_send(w, js):
        k, g, lo = order(w)

        @pl.when(is_src)
        def _():
            for j in js:
                yy = yplus(YOFF[j])
                for d in range(2):
                    rcopy(S[k].at[g, y % 2, lo, yy], R[k].at[g, x // 2, lo, yy],
                          xs.at[k], xr.at[w, j if j % 2 == d else 4], dev(x=xplus(side(d)))).start()

    def x_rest(w):
        k, g, lo = order(w)

        @pl.when(is_src)
        def _():
            for pos in range(4):
                for d in range(2):
                    j = ((0, 2, 1, 3), (1, 3, 0, 2))[d][pos]
                    yy = yplus(YOFF[j])
                    rcopy(S[k].at[g, y % 2, lo, yy], R[k].at[g, x // 2, lo, yy],
                          xs.at[k], xr.at[w, j if j % 2 == d else 4], dev(x=xplus(side(d)))).start()

    def x_local(w):
        k, g, lo = order(w)

        @pl.when(is_src)
        def _():
            pltpu.make_async_copy(S[k].at[g, y % 2, lo], R[k].at[g, x // 2, lo], ls.at[w]).start()

    def x_fwd(w, js=(0, 1, 2, 3)):
        k, g, lo = order(w)

        @pl.when(is_mid)
        def _():
            for j in js:
                d = j % 2
                unit = R[k].at[g, xplus(4 - side(d)) // 2, lo, yplus(YOFF[j])]
                got(unit, xr.at[w, j])
                rcopy(unit, unit, gs.at[k], gr.at[w], dev(x=xplus(side(d)))).start()

    def x_last(w):
        k, g, lo = order(w)

        @pl.when(is_src)
        def _():
            got(R[k].at[g, 1 - x // 2, lo], gr.at[w])
            own = R[k].at[g, x // 2, lo]
            pltpu.make_async_copy(own, own, ls.at[w]).wait()

        @pl.when(is_mid)
        def _():
            got(R[k].at[g, 0, lo], xr.at[w, 4])

    def psum_own(k):
        def body(i, carry):
            block = S[k][i // 4, (i // 2) % 2, i % 2, y].astype(jnp.float32)
            return carry + (block[0:8] + block[8:16]) + (block[16:24] + block[24:32])

        total8 = lax.fori_loop(0, 8, body, jnp.zeros((8, widths[k]), jnp.float32))
        psx[k][x] = jnp.sum(total8, axis=0, keepdims=True)
        for d in (1, 2, 3):
            c = rcopy(psx[k].at[x], psx[k].at[x], pxs.at[k], pxr.at[k], dev(x=xplus(d)))
            c.start()

    def psum_x(k):
        got(psx[k].at[0:3], pxr.at[k])
        psy[k][y] = (psx[k][0] + psx[k][1]) + (psx[k][2] + psx[k][3])
        for d in (1, 2, 3):
            c = rcopy(psy[k].at[y], psy[k].at[y], pys.at[k], pyr.at[k], dev(y=yplus(d)))
            c.start()

    def psum_y(k):
        got(psy[k].at[0:3], pyr.at[k])
        mean[k][...] = ((psy[k][0] + psy[k][1]) + (psy[k][2] + psy[k][3])) / snaps

    def scaled(k, block):
        return ((block.astype(jnp.float32) - mean[k][...]) * fac[k][...]).astype(jnp.bfloat16)

    def scale_s(w):
        k, g, lo = order(w)

        def body(i, carry):
            at = g * 512 + (i // 4) * 256 + lo * 128 + (i % 4) * 32
            Sc[k][pl.ds(pl.multiple_of(at, 32), 32), :] = scaled(k, S[k][g, i // 4, lo, i % 4])
            return carry

        lax.fori_loop(0, 8, body, 0)

    def multiply(w):
        k, g, lo = order(w)

        def body(i, carry):
            Rc[k][pl.ds(pl.multiple_of(i * 32, 32), 32), :] = scaled(k, R[k][g, i // 4, lo, i % 4])
            return carry

        lax.fori_loop(0, 8, body, 0)

        def dot(zo, carry):
            product = lax.dot_general(
                Rc[k][...], Sc[k][pl.ds(zo * 512 if isinstance(zo, int) else pl.multiple_of(zo * 512, 512), 512), :],
                (((1,), (1,)), ((), ())), preferred_element_type=jnp.float32)
            if k == 0:
                part[lo, g, zo] = product.reshape(2, 2, 64, 512)
            else:
                part[lo, g, zo] += product.reshape(2, 2, 64, 512)
            return carry

        if k == 0:
            lax.fori_loop(0, 2, dot, 0)
        else:
            for zo in range(2):
                dot(zo, 0)
                give(lo, g, zo)

    def give(lo, g, zo):
        rcopy(part.at[lo, g, zo, :, 1 - core], xbuf.at[lo, g, zo], cs, cr.at[lo, g, zo], dev(core=1 - core)).start()

    def piece(lo, dz, half, sub):
        zz, rows = zplus(dz), 32 // SUBS[lo]
        return part.at[lo, zz // 4, zz % 2, (zz // 2) % 2, core, pl.ds(half * 32 + sub * rows, rows), :]

    def tr_send(lo, steps, half, sub, upward):
        ss, sr, buf, fr_, fb = (us, ur, up, eur, eup) if upward else (ds, dr, down, edr, edown)
        src, z_t = piece(lo, steps if upward else 8 - steps, half, sub), zplus(1 if upward else 7)
        if steps > 1:
            slot = ((steps - 2) * 2 + half) * SUBS[lo] + sub
            rcopy(src, buf[lo].at[slot], ss, sr[lo].at[slot], dev(z=z_t)).start()
        else:
            rows, n = 32 // SUBS[lo], half * SUBS[lo] + sub
            rcopy(src, fb.at[core, pl.ds(half * 32 + sub * rows, rows), :], ss, fr_.at[core, n], dev(z=z_t, core=lo)).start()

    def tr_pass(lo, steps, half, upward):
        sr, buf = (ur, up) if upward else (dr, down)

        def one(sub):
            slot = ((steps - 1) * 2 + half) * SUBS[lo] + sub
            got(buf[lo].at[slot], sr[lo].at[slot])
            mine = piece(lo, steps if upward else 8 - steps, half, sub)
            mine[...] += buf[lo][slot]
            tr_send(lo, steps, half, sub, upward)

        return one

    def tr_start(lo):
        for g in range(2):
            for zo in range(2):
                got(xbuf.at[lo, g, zo], cr.at[lo, g, zo])
                part[lo, g, zo, :, core] += xbuf[lo, g, zo]
        for steps, half in ((4, 0), (3, 1)):
            for sub in range(SUBS[lo]):
                tr_send(lo, steps, half, sub, True)
                tr_send(lo, steps, 1 - half, sub, False)

        @pl.when(core != lo)
        def _():
            rcopy(part.at[lo, z // 4, zlo, (z // 2) % 2, core], obuf, os, orr, dev(core=1 - core)).start()

    def tr_step(lo, steps):
        for st, half in ((steps, 0), (steps - 1, 1)):
            if st > 0:
                for sub in range(SUBS[lo]):
                    tr_pass(lo, st, half, True)(sub)
                    tr_pass(lo, st, 1 - half, False)(sub)

    def tr_end(lo):
        @pl.when(core == lo)
        def _():
            got(obuf, orr)
            for c in range(2):
                for n in range(2 * SUBS[lo]):
                    rows = 32 // SUBS[lo]
                    got(eup.at[c, n * rows:(n + 1) * rows, :], eur.at[c, n])
                    got(edown.at[c, n * rows:(n + 1) * rows, :], edr.at[c, n])
            mine = part[lo, z // 4, zlo, (z // 2) % 2, lo]
            o_ref[lo * 64:(lo + 1) * 64, :] = mine + eup[lo] + edown[lo]
            o_ref[(1 - lo) * 64:(2 - lo) * 64, :] = obuf[...] + eup[1 - lo] + edown[1 - lo]

    def drain():
        for k in range(PARTS):
            left(Sc[k].at[0:240], a_s.at[k])
            left(S[k].at[0], ys.at[k])
            left(S[k].at[0, 0], fs.at[k])
            left(psx[k].at[0:3], pxs.at[k])
            left(psy[k].at[0:3], pys.at[k])

            @pl.when(is_src)
            def _(k=k):
                left(S[k], xs.at[k])

            @pl.when(is_mid)
            def _(k=k):
                left(S[k].at[0], gs.at[k])

        left(xbuf, cs)
        left(Sc[0].at[0:448], us)
        left(Sc[0].at[0:448], ds)
        left(obuf, os)

    a_wait(0)
    y_own(0)
    x_send(0, (0,))
    tr_weights()
    a_wait(1)
    y_own(1)
    x_send(1, (0,))
    y_wait(0)
    x_send(0, (1, 2))
    a_wait(2)
    y_own(2)
    x_send(2, (0,))
    y_wait(1)
    x_send(1, (1, 2))
    a_wait(3)
    tr_cells_late()
    y_own(3)
    x_send(3, (0,))
    psum_own(0)
    y_last(0)
    x_send(0, (3,))
    x_local(0)
    y_wait(2)
    x_send(2, (1, 2))
    a_wait(4)
    y_own(4)
    x_send(4, (0,))
    y_last(1)
    x_send(1, (3,))
    x_local(1)
    psum_x(0)
    y_wait(3)
    a_wait(5)
    y_own(5)
    x_fwd(0)
    y_last(2)
    x_send(2, (3,))
    x_local(2)
    y_wait(4)
    x_send(4, (1, 2))
    a_wait(6)
    y_own(6)
    x_send(5, (0,))
    psum_y(0)
    y_last(3)
    x_local(3)
    a_wait(7)
    psum_own(1)
    x_fwd(1)
    y_wait(5)
    x_send(5, (1, 2))
    y_own(7)
    scale_s(0)
    scale_s(1)
    scale_s(2)
    scale_s(3)
    y_last(4)
    x_send(4, (3,))
    x_local(4)
    x_fwd(2)
    x_fwd(4, (0, 1, 2))
    x_last(0)
    multiply(0)
    y_wait(6)
    y_last(5)
    x_send(5, (3,))
    x_local(5)
    x_send(3, (1, 2, 3))
    x_fwd(5, (0, 1, 2))
    x_last(1)
    multiply(1)
    x_fwd(4, (3,))
    psum_x(1)
    y_wait(7)
    x_fwd(5, (3,))
    y_last(6)
    x_rest(6)
    x_local(6)
    x_last(2)
    multiply(2)
    psum_y(1)
    scale_s(4)
    scale_s(5)
    scale_s(6)
    y_last(7)
    x_rest(7)
    x_local(7)
    scale_s(7)
    x_last(4)
    multiply(4)
    x_fwd(3)
    x_last(5)
    multiply(5)
    tr_start(0)
    x_last(3)
    multiply(3)
    x_fwd(6)
    tr_step(0, 3)
    x_fwd(7)
    x_last(6)
    multiply(6)
    tr_step(0, 2)
    x_last(7)
    multiply(7)
    tr_step(0, 1)
    tr_start(1)
    tr_step(1, 3)
    tr_step(1, 2)
    tr_step(1, 1)
    tr_end(0)
    tr_end(1)
    drain()


def solution(mesh):
    def on_device(snapshots, cell_weights):
        per_device, cells = snapshots.shape
        snaps = per_device * mesh.shape["row"] * mesh.shape["col"]
        widths = (FIRST, cells // 16 - FIRST)
        dma, bf16, f32 = pltpu.SemaphoreType.DMA, jnp.bfloat16, jnp.float32
        V = pltpu.VMEM
        return pl.pallas_call(
            functools.partial(kernel, snaps, cells),
            out_shape=jax.ShapeDtypeStruct((128, 512), f32),
            in_specs=[pl.BlockSpec(memory_space=pl.ANY), pl.BlockSpec(memory_space=pl.ANY)],
            out_specs=pl.BlockSpec(memory_space=V),
            scratch_shapes=[
                [V((2, 2, 2, 4, 32, n), bf16) for n in widths],
                [V((2, 2, 2, 4, 32, n), bf16) for n in widths],
                [V((1024, n), bf16) for n in widths],
                [V((256, n), bf16) for n in widths],
                [V((4, 1, n), f32) for n in widths],
                [V((4, 1, n), f32) for n in widths],
                [V((1, n), f32) for n in widths],
                [V((1, n), f32) for n in widths],
                V((2, 2, 2, 2, 2, 64, 512), f32),
                V((2, 2, 2, 2, 64, 512), f32),
                [V((6 * n, 32 // n, 512), f32) for n in SUBS],
                [V((6 * n, 32 // n, 512), f32) for n in SUBS],
                V((2, 64, 512), f32),
                V((2, 64, 512), f32),
                V((64, 512), f32),
                V((cells // 128, 128), f32),
                dma((PARTS,)), dma((PARTS, 4)),
                dma((PARTS,)), dma((ROUNDS, 2)), dma((PARTS,)), dma((ROUNDS,)),
                dma((PARTS,)), dma((ROUNDS, 5)), dma((PARTS,)), dma((ROUNDS,)),
                dma((PARTS,)), dma((PARTS,)), dma((PARTS,)), dma((PARTS,)),
                dma, dma((2, 2, 2)), dma, [dma((6 * n,)) for n in SUBS], dma, [dma((6 * n,)) for n in SUBS],
                dma((2, 2 * max(SUBS))), dma((2, 2 * max(SUBS))), dma, dma,
                dma((ROUNDS,)), dma,
            ],
            compiler_params=pltpu.CompilerParams(
                collective_id=0, has_side_effects=True, vmem_limit_bytes=60 * 1024 * 1024),
        )(snapshots, cell_weights.reshape(cells // 128, 128))

    return jax.shard_map(
        on_device,
        mesh=mesh,
        in_specs=(P(("row", "col"), None), P()),
        out_specs=P("col", "row"),
        check_vma=False,
    )
```

```python
import functools

import jax
import jax.numpy as jnp
from jax import lax
from jax.experimental import pallas as pl
from jax.experimental.pallas import tpu as pltpu
from jax.sharding import PartitionSpec as P

MESH = pl.DeviceIdType.MESH
YOFF = (0, 3, 1, 2)
PARTS = 2
FIRST = 1024
SUBS = (2, 2)
ROUNDS = 4 * PARTS


def kernel(snaps, cells, x_ref, w_hbm, o_ref, S, R, Sc, Rc, psx, psy, mean, fac, part, xbuf, up, down, eup, edown, obuf, w_ref,
           a_s, a_r, ys, yr, fs, fr, xs, xr, gs, gr, pxs, pxr, pys, pyr, cs, cr, us, ur, ds, dr, eur, edr, os, orr, ls, ws):
    slab = cells // 16
    widths = (FIRST, slab - FIRST)
    row, col = lax.axis_index("row"), lax.axis_index("col")
    zlo, x = row // 4, row % 4
    zhi, y, core = col // 8, (col // 2) % 4, col % 2
    z = zhi * 2 + zlo
    is_src = (x % 2) == (y // 2)
    is_mid = jnp.logical_not(is_src)

    def dev(z=z, x=x, y=y, core=core):
        return ((z % 2) * 4 + x, (z // 2) * 8 + y * 2 + core)

    def xplus(d):
        return (x + d) % 4

    def yplus(d):
        return (y + d) % 4

    def zplus(d):
        return (z + d) % 8

    def side(d):
        return 1 if d == 0 else 3

    def rcopy(src, dst, ssem, rsem, device):
        return pltpu.make_async_remote_copy(src_ref=src, dst_ref=dst, send_sem=ssem, recv_sem=rsem,
                                            device_id=device, device_id_type=MESH)

    def got(ref, rsem):
        rcopy(ref, ref, a_s.at[0], rsem, dev(core=1 - core)).wait_recv()

    def left(ref, ssem):
        rcopy(ref, ref, ssem, a_r.at[0, 0], dev(core=1 - core)).wait_send()


    weights = pltpu.make_async_copy(w_hbm, w_ref, ws)
    weights.start()

    barrier = pltpu.get_barrier_semaphore()
    peers = []
    for dz in (4, 3, 5, 2, 6, 1, 7, 0):
        for dc in range(2):
            if dz or dc:
                peers.append(dev(z=zplus(dz), core=(core + dc) % 2))
    peers += [dev(y=yplus(d)) for d in (2, 1, 3)] + [dev(x=xplus(d)) for d in (2, 1, 3)]

    def barrier_all():
        for peer in peers:
            pl.semaphore_signal(barrier, inc=1, device_id=peer, device_id_type=MESH)
        pl.semaphore_wait(barrier, len(peers))

    barrier_all()

    late_lo = (z + 1) // 2 % 2

    def order(w):
        part_of, v = w // 4, w % 4
        m = (z + (2, 0, 1 + 2 * late_lo, 3 - 2 * late_lo)[v]) % 4 if part_of < PARTS - 1 else v
        return part_of, m % 2, m // 2

    me_slot = z * 2 + core

    def tr_cells(k):
        block = S[k].at[zlo, zhi // 2, zhi % 2, y, pl.ds(pl.multiple_of(core * 16, 16), 16), :]
        for dz in (6, 2, 0, 4, 7, 3, 1, 5):
            for dc in range(2):
                z_t, core_t = zplus(dz), (core + dc) % 2
                first = (z_t * 2 + core_t) * slab + k * FIRST
                src = x_ref.at[:, pl.ds(pl.multiple_of(first, 128), widths[k])]
                if dz == 0 and dc == 0:
                    pltpu.make_async_copy(src, block, a_r.at[k, z % 4]).start()
                else:
                    rcopy(src, block, a_s.at[k], a_r.at[k, z % 4], dev(z=z_t, core=core_t)).start()

    late = z % 4 >= 2

    def tr_cells_late():
        @pl.when(late)
        def _():
            tr_cells(1)

    tr_cells(0)

    @pl.when(jnp.logical_not(late))
    def _():
        tr_cells(1)

    def tr_weights():
        weights.wait()
        total = jnp.sum(w_ref[...])
        scale = jnp.sqrt(w_ref[pl.ds(pl.multiple_of(me_slot * 16, 16), 16), :] / total)
        for j in range(16):
            k, at = (0, j * 128) if j * 128 < FIRST else (1, j * 128 - FIRST)
            fac[k][:, at:at + 128] = scale[j:j + 1, :]

    def a_wait(w):
        k, g, lo = order(w)
        got(S[k].at[g, :, lo, y], a_r.at[k, 2 * lo + g])

    def y_own(w):
        k, g, lo = order(w)
        unit = S[k].at[g, :, lo, y]
        for d in range(2):
            rcopy(unit, unit, ys.at[k], yr.at[w, d], dev(y=yplus(side(d)))).start()

    def y_wait(w):
        k, g, lo = order(w)
        for d in range(2):
            yy = yplus(4 - side(d))
            got(S[k].at[g, :, lo, yy], yr.at[w, d])
            half = S[k].at[g, d, lo, yy]
            rcopy(half, half, fs.at[k], fr.at[w], dev(y=yplus(side(d)))).start()

    def y_last(w):
        k, g, lo = order(w)
        got(S[k].at[g, :, lo, yplus(2)], fr.at[w])

    def x_send(w, js):
        k, g, lo = order(w)

        @pl.when(is_src)
        def _():
            for j in js:
                yy = yplus(YOFF[j])
                for d in range(2):
                    rcopy(S[k].at[g, y % 2, lo, yy], R[k].at[g, x // 2, lo, yy],
                          xs.at[k], xr.at[w, j if j % 2 == d else 4], dev(x=xplus(side(d)))).start()

    def x_rest(w):
        k, g, lo = order(w)

        @pl.when(is_src)
        def _():
            for pos in range(4):
                for d in range(2):
                    j = ((0, 2, 1, 3), (1, 3, 0, 2))[d][pos]
                    yy = yplus(YOFF[j])
                    rcopy(S[k].at[g, y % 2, lo, yy], R[k].at[g, x // 2, lo, yy],
                          xs.at[k], xr.at[w, j if j % 2 == d else 4], dev(x=xplus(side(d)))).start()

    def x_local(w):
        k, g, lo = order(w)

        @pl.when(is_src)
        def _():
            pltpu.make_async_copy(S[k].at[g, y % 2, lo], R[k].at[g, x // 2, lo], ls.at[w]).start()

    def x_fwd(w, js=(0, 1, 2, 3)):
        k, g, lo = order(w)

        @pl.when(is_mid)
        def _():
            for j in js:
                d = j % 2
                unit = R[k].at[g, xplus(4 - side(d)) // 2, lo, yplus(YOFF[j])]
                got(unit, xr.at[w, j])
                rcopy(unit, unit, gs.at[k], gr.at[w], dev(x=xplus(side(d)))).start()

    def x_last(w):
        k, g, lo = order(w)

        @pl.when(is_src)
        def _():
            got(R[k].at[g, 1 - x // 2, lo], gr.at[w])
            own = R[k].at[g, x // 2, lo]
            pltpu.make_async_copy(own, own, ls.at[w]).wait()

        @pl.when(is_mid)
        def _():
            got(R[k].at[g, 0, lo], xr.at[w, 4])

    def psum_own(k):
        def body(i, carry):
            block = S[k][i // 4, (i // 2) % 2, i % 2, y].astype(jnp.float32)
            return carry + (block[0:8] + block[8:16]) + (block[16:24] + block[24:32])

        total8 = lax.fori_loop(0, 8, body, jnp.zeros((8, widths[k]), jnp.float32))
        psx[k][x] = jnp.sum(total8, axis=0, keepdims=True)
        for d in (1, 2, 3):
            c = rcopy(psx[k].at[x], psx[k].at[x], pxs.at[k], pxr.at[k], dev(x=xplus(d)))
            c.start()

    def psum_x(k):
        got(psx[k].at[0:3], pxr.at[k])
        psy[k][y] = (psx[k][0] + psx[k][1]) + (psx[k][2] + psx[k][3])
        for d in (1, 2, 3):
            c = rcopy(psy[k].at[y], psy[k].at[y], pys.at[k], pyr.at[k], dev(y=yplus(d)))
            c.start()

    def psum_y(k):
        got(psy[k].at[0:3], pyr.at[k])
        mean[k][...] = ((psy[k][0] + psy[k][1]) + (psy[k][2] + psy[k][3])) / snaps

    def scaled(k, block):
        return ((block.astype(jnp.float32) - mean[k][...]) * fac[k][...]).astype(jnp.bfloat16)

    def scale_s(w):
        k, g, lo = order(w)

        def body(i, carry):
            at = g * 512 + (i // 4) * 256 + lo * 128 + (i % 4) * 32
            Sc[k][pl.ds(pl.multiple_of(at, 32), 32), :] = scaled(k, S[k][g, i // 4, lo, i % 4])
            return carry

        lax.fori_loop(0, 8, body, 0)

    def multiply(w):
        k, g, lo = order(w)

        def body(i, carry):
            Rc[k][pl.ds(pl.multiple_of(i * 32, 32), 32), :] = scaled(k, R[k][g, i // 4, lo, i % 4])
            return carry

        lax.fori_loop(0, 8, body, 0)

        def dot(zo, carry):
            product = lax.dot_general(
                Rc[k][...], Sc[k][pl.ds(zo * 512 if isinstance(zo, int) else pl.multiple_of(zo * 512, 512), 512), :],
                (((1,), (1,)), ((), ())), preferred_element_type=jnp.float32)
            if k == 0:
                part[lo, g, zo] = product.reshape(2, 2, 64, 512)
            else:
                part[lo, g, zo] += product.reshape(2, 2, 64, 512)
            return carry

        if k == 0:
            lax.fori_loop(0, 2, dot, 0)
        else:
            for zo in range(2):
                dot(zo, 0)
                give(lo, g, zo)

    def give(lo, g, zo):
        rcopy(part.at[lo, g, zo, :, 1 - core], xbuf.at[lo, g, zo], cs, cr.at[lo, g, zo], dev(core=1 - core)).start()

    def piece(lo, dz, half, sub):
        zz, rows = zplus(dz), 32 // SUBS[lo]
        return part.at[lo, zz // 4, zz % 2, (zz // 2) % 2, core, pl.ds(half * 32 + sub * rows, rows), :]

    def tr_send(lo, steps, half, sub, upward):
        ss, sr, buf, fr_, fb = (us, ur, up, eur, eup) if upward else (ds, dr, down, edr, edown)
        src, z_t = piece(lo, steps if upward else 8 - steps, half, sub), zplus(1 if upward else 7)
        if steps > 1:
            slot = ((steps - 2) * 2 + half) * SUBS[lo] + sub
            rcopy(src, buf[lo].at[slot], ss, sr[lo].at[slot], dev(z=z_t)).start()
        else:
            rows, n = 32 // SUBS[lo], half * SUBS[lo] + sub
            rcopy(src, fb.at[core, pl.ds(half * 32 + sub * rows, rows), :], ss, fr_.at[core, n], dev(z=z_t, core=lo)).start()

    def tr_pass(lo, steps, half, upward):
        sr, buf = (ur, up) if upward else (dr, down)

        def one(sub):
            slot = ((steps - 1) * 2 + half) * SUBS[lo] + sub
            got(buf[lo].at[slot], sr[lo].at[slot])
            mine = piece(lo, steps if upward else 8 - steps, half, sub)
            mine[...] += buf[lo][slot]
            tr_send(lo, steps, half, sub, upward)

        return one

    def tr_start(lo):
        for g in range(2):
            for zo in range(2):
                got(xbuf.at[lo, g, zo], cr.at[lo, g, zo])
                part[lo, g, zo, :, core] += xbuf[lo, g, zo]
        for steps, half in ((4, 0), (3, 1)):
            for sub in range(SUBS[lo]):
                tr_send(lo, steps, half, sub, True)
                tr_send(lo, steps, 1 - half, sub, False)

        @pl.when(core != lo)
        def _():
            rcopy(part.at[lo, z // 4, zlo, (z // 2) % 2, core], obuf, os, orr, dev(core=1 - core)).start()

    def tr_step(lo, steps):
        for st, half in ((steps, 0), (steps - 1, 1)):
            if st > 0:
                for sub in range(SUBS[lo]):
                    tr_pass(lo, st, half, True)(sub)
                    tr_pass(lo, st, 1 - half, False)(sub)

    def tr_end(lo):
        @pl.when(core == lo)
        def _():
            got(obuf, orr)
            for c in range(2):
                for n in range(2 * SUBS[lo]):
                    rows = 32 // SUBS[lo]
                    got(eup.at[c, n * rows:(n + 1) * rows, :], eur.at[c, n])
                    got(edown.at[c, n * rows:(n + 1) * rows, :], edr.at[c, n])
            mine = part[lo, z // 4, zlo, (z // 2) % 2, lo]
            o_ref[lo * 64:(lo + 1) * 64, :] = mine + eup[lo] + edown[lo]
            o_ref[(1 - lo) * 64:(2 - lo) * 64, :] = obuf[...] + eup[1 - lo] + edown[1 - lo]

    def drain():
        for k in range(PARTS):
            left(Sc[k].at[0:240], a_s.at[k])
            left(S[k].at[0], ys.at[k])
            left(S[k].at[0, 0], fs.at[k])
            left(psx[k].at[0:3], pxs.at[k])
            left(psy[k].at[0:3], pys.at[k])

            @pl.when(is_src)
            def _(k=k):
                left(S[k], xs.at[k])

            @pl.when(is_mid)
            def _(k=k):
                left(S[k].at[0], gs.at[k])

        left(xbuf, cs)
        left(Sc[0].at[0:448], us)
        left(Sc[0].at[0:448], ds)
        left(obuf, os)

    a_wait(0)
    y_own(0)
    x_send(0, (0,))
    tr_weights()
    a_wait(1)
    y_own(1)
    x_send(1, (0,))
    y_wait(0)
    x_send(0, (1, 2))
    a_wait(2)
    y_own(2)
    x_send(2, (0,))
    y_wait(1)
    x_send(1, (1, 2))
    a_wait(3)
    tr_cells_late()
    y_own(3)
    x_send(3, (0,))
    psum_own(0)
    y_last(0)
    x_send(0, (3,))
    x_local(0)
    y_wait(2)
    x_send(2, (1, 2))
    a_wait(4)
    y_own(4)
    x_send(4, (0,))
    y_last(1)
    x_send(1, (3,))
    x_local(1)
    psum_x(0)
    y_wait(3)
    a_wait(5)
    y_own(5)
    x_fwd(0)
    y_last(2)
    x_send(2, (3,))
    x_local(2)
    y_wait(4)
    x_send(4, (1, 2))
    a_wait(6)
    y_own(6)
    x_send(5, (0,))
    psum_y(0)
    y_last(3)
    x_local(3)
    a_wait(7)
    psum_own(1)
    x_fwd(1)
    y_wait(5)
    x_send(5, (1, 2))
    y_own(7)
    scale_s(0)
    scale_s(1)
    scale_s(2)
    scale_s(3)
    y_last(4)
    x_send(4, (3,))
    x_local(4)
    x_fwd(2)
    x_fwd(4, (0, 1, 2))
    x_last(0)
    multiply(0)
    y_wait(6)
    y_last(5)
    x_send(5, (3,))
    x_local(5)
    x_send(3, (1, 2, 3))
    x_fwd(5, (0, 1, 2))
    x_last(1)
    multiply(1)
    x_fwd(4, (3,))
    psum_x(1)
    y_wait(7)
    x_fwd(5, (3,))
    y_last(6)
    x_rest(6)
    x_local(6)
    x_last(2)
    multiply(2)
    psum_y(1)
    scale_s(4)
    scale_s(5)
    scale_s(6)
    y_last(7)
    x_rest(7)
    x_local(7)
    scale_s(7)
    x_fwd(3, (0, 1))
    x_last(4)
    multiply(4)
    x_fwd(3, (2, 3))
    x_last(5)
    multiply(5)
    tr_start(0)
    x_fwd(6, (0, 1))
    x_last(3)
    multiply(3)
    x_fwd(6, (2, 3))
    x_fwd(7, (0, 1))
    tr_step(0, 3)
    x_fwd(7, (2, 3))
    x_last(6)
    multiply(6)
    tr_step(0, 2)
    x_last(7)
    multiply(7)
    tr_step(0, 1)
    tr_start(1)
    tr_step(1, 3)
    tr_step(1, 2)
    tr_step(1, 1)
    tr_end(0)
    tr_end(1)
    drain()


def solution(mesh):
    def on_device(snapshots, cell_weights):
        per_device, cells = snapshots.shape
        snaps = per_device * mesh.shape["row"] * mesh.shape["col"]
        widths = (FIRST, cells // 16 - FIRST)
        dma, bf16, f32 = pltpu.SemaphoreType.DMA, jnp.bfloat16, jnp.float32
        V = pltpu.VMEM
        return pl.pallas_call(
            functools.partial(kernel, snaps, cells),
            out_shape=jax.ShapeDtypeStruct((128, 512), f32),
            in_specs=[pl.BlockSpec(memory_space=pl.ANY), pl.BlockSpec(memory_space=pl.ANY)],
            out_specs=pl.BlockSpec(memory_space=V),
            scratch_shapes=[
                [V((2, 2, 2, 4, 32, n), bf16) for n in widths],
                [V((2, 2, 2, 4, 32, n), bf16) for n in widths],
                [V((1024, n), bf16) for n in widths],
                [V((256, n), bf16) for n in widths],
                [V((4, 1, n), f32) for n in widths],
                [V((4, 1, n), f32) for n in widths],
                [V((1, n), f32) for n in widths],
                [V((1, n), f32) for n in widths],
                V((2, 2, 2, 2, 2, 64, 512), f32),
                V((2, 2, 2, 2, 64, 512), f32),
                [V((6 * n, 32 // n, 512), f32) for n in SUBS],
                [V((6 * n, 32 // n, 512), f32) for n in SUBS],
                V((2, 64, 512), f32),
                V((2, 64, 512), f32),
                V((64, 512), f32),
                V((cells // 128, 128), f32),
                dma((PARTS,)), dma((PARTS, 4)),
                dma((PARTS,)), dma((ROUNDS, 2)), dma((PARTS,)), dma((ROUNDS,)),
                dma((PARTS,)), dma((ROUNDS, 5)), dma((PARTS,)), dma((ROUNDS,)),
                dma((PARTS,)), dma((PARTS,)), dma((PARTS,)), dma((PARTS,)),
                dma, dma((2, 2, 2)), dma, [dma((6 * n,)) for n in SUBS], dma, [dma((6 * n,)) for n in SUBS],
                dma((2, 2 * max(SUBS))), dma((2, 2 * max(SUBS))), dma, dma,
                dma((ROUNDS,)), dma,
            ],
            compiler_params=pltpu.CompilerParams(
                collective_id=0, has_side_effects=True, vmem_limit_bytes=60 * 1024 * 1024),
        )(snapshots, cell_weights.reshape(cells // 128, 128))

    return jax.shard_map(
        on_device,
        mesh=mesh,
        in_specs=(P(("row", "col"), None), P()),
        out_specs=P("col", "row"),
        check_vma=False,
    )
```
